512 devices in a mesh: dp: 16 (over x, y_lo, core), ctx: 32 (over z, y_hi).
Axes of the slice: x: 4, y: 4 (y_hi: 2, y_lo: 2; y = y_hi * 2 + y_lo), z: 16, core: 2. Of those that a mesh axis runs over, the one named last changes fastest.
Arguments:
- values: bfloat16 [16, 4096, 4096], P('dp', 'ctx'), may hold values from -6 to 6
- gate_values: bfloat16 [16, 4096, 4096], P('dp', 'ctx'), may hold values from -6 to 6
- cotangent: bfloat16 [16, 4096, 4096], P('dp', 'ctx'), may hold values from -6 to 6
- residues: float32 [8, 4096], replicated, may hold values from -0.3 to 0.3
- decay_rates: float32 [8, 4096], replicated, may hold values from 2.4414063e-05 to 0.1
Outputs:
- input_grad: bfloat16 [16, 4096, 4096], P('dp', 'ctx')
- resid_grad: float32 [8, 4096], replicated
- decay_grad: float32 [8, 4096], replicated
The draws below stay inside these ranges and needn't reach their ends.
All inputs are finite; a program needn't handle non-finite values.
Results may differ from the reference program's by a relative error of at most 0.0013.
Values sent between devices are 32-bit elements; how exact they have to be, the bound alone decides.
No kernel may reach another device: no remote copies, remote signals or barrier semaphores. Data moves between devices by JAX's collectives and lax.ppermute only.
A program may use at most 64 MiB of HBM per device.

```python
import math
import jax
import jax.numpy as jnp
from jax import lax

C = 4096
NSTATE = 8
LEN = 4096
SEQS = 16


def steps_of(own_key, extent, shards, least, largest):
    loudness = 1.0
    for dim, shards_of in shards:
        heights = jax.random.uniform(jax.random.fold_in(jax.random.fold_in(own_key, 6), dim), (shards_of,), jnp.float32, least / len(shards), largest / len(shards))
        loudness = loudness * jnp.repeat(jnp.exp(heights), extent[dim] // shards_of).reshape((-1,) + (1,) * (len(extent) - 1 - dim))
    return loudness


def centred(key, extent, deviation, limit, split=(), kind=jnp.bfloat16):
    values = jax.random.normal(key, extent, jnp.float32) * deviation
    if len(split) > 0:
        values = steps_of(key, extent, split, -0.22, 0.18) * values
    return jnp.clip(values, min=-limit, max=limit).astype(kind)


def setup_inputs(seed: int = 0) -> dict:
    splits = jax.random.split(jax.random.key(seed), 6)
    values = centred(splits[0], (SEQS, LEN, C), 1.0, 6.0, ((0, 16), (1, 32)))
    gate_values = centred(splits[1], (SEQS, LEN, C), 1.0, 6.0, ((0, 16), (1, 32)))
    cotangent = centred(splits[2], (SEQS, LEN, C), 1.0, 6.0, ((0, 16), (1, 32)))
    residues = centred(splits[3], (NSTATE, C), 0.05, 0.3, (), jnp.float32)
    decay_rates = jnp.clip(jnp.exp(jax.random.uniform(splits[4], (NSTATE, C), jnp.float32, math.log(2.441406286379788e-05), math.log(0.1))), 2.441406286379788e-05, 0.1)
    return {"values": values, "gate_values": gate_values, "cotangent": cotangent, "residues": residues, "decay_rates": decay_rates}


def reference(values, gate_values, cotangent, residues, decay_rates):
    factor = jnp.exp(-decay_rates)
    seq_values = jnp.swapaxes(values, 0, 1)
    seq_grad = jnp.swapaxes(cotangent.astype(jnp.float32) * gate_values.astype(jnp.float32), 0, 1)
    empty = jnp.zeros((values.shape[0], residues.shape[0], values.shape[2]), jnp.float32)
    flat = jnp.zeros(residues.shape, jnp.float32)

    def forward_step(carry, inputs):
        state_now, moment_now, sum_state, sum_moment = carry
        value_now, grad_now = inputs
        moment_now = factor * (moment_now + state_now)
        state_now = factor * state_now + value_now.astype(jnp.float32)[:, None, :]
        weight_now = grad_now[:, None, :]
        sum_state = sum_state + lax.optimization_barrier(jnp.sum(weight_now * state_now, axis=0))
        sum_moment = sum_moment + lax.optimization_barrier(jnp.sum(weight_now * moment_now, axis=0))
        return ((state_now, moment_now, sum_state, sum_moment), None)
    outcome, _ = lax.scan(forward_step, (empty, empty, flat, flat), (seq_values, seq_grad))

    def backward_step(back_now, grad_now):
        back_now = factor * back_now + grad_now[:, None, :]
        return (back_now, lax.optimization_barrier(jnp.sum(residues * back_now, axis=1)))
    _, grad_rows = lax.scan(backward_step, empty, seq_grad, reverse=True)
    scale = 1.0 / math.sqrt(SEQS * LEN)
    input_grad = jnp.swapaxes(grad_rows, 0, 1).astype(jnp.bfloat16)
    resid_grad = outcome[2] * scale
    decay_grad = -decay_rates * residues * outcome[3] * scale
    return (input_grad, resid_grad, decay_grad)
```

```python
import functools
import math

import jax
import jax.numpy as jnp
from jax import lax
from jax.experimental import pallas as pl
from jax.experimental.pallas import tpu as pltpu
from jax.sharding import PartitionSpec as P

F32 = jnp.float32
LANES = 128
SUBS = 8
WIDE = LANES * SUBS
NEAR = 4
SENT = 6
BACK = 3
UNROLL = 4


def rows(start, size):
    return pl.ds(pl.multiple_of(start, size), size)


def split_columns(read, scratch, length):
    for s in range(SUBS):
        scratch[pl.ds(s, length, stride=SUBS), :] = read(slice(s * LANES, (s + 1) * LANES))


def local_kernel(length, modes, values, gate, cotangent, decay, grad, sent, value_rows, decay_rows):
    split_columns(lambda c: values[0, :, c].astype(F32), value_rows, length)
    split_columns(
        lambda c: cotangent[0, :, c].astype(F32) * gate[0, :, c].astype(F32), grad, length
    )
    split_columns(lambda c: decay[:, c], decay_rows, modes)
    factor = [jnp.exp(-decay_rows[n * SUBS : (n + 1) * SUBS, :]) for n in range(modes)]
    zero = [jnp.zeros((SUBS, LANES), F32)] * modes

    def forward(t, carry):
        state, moment, sum0, sum1 = (list(part) for part in carry)
        value_now = value_rows[rows(t * SUBS, SUBS), :]
        grad_now = grad[rows(t * SUBS, SUBS), :]
        for n in range(modes):
            moment[n] = factor[n] * (moment[n] + state[n])
            state[n] = factor[n] * state[n] + value_now
            sum0[n] = sum0[n] + grad_now * state[n]
            sum1[n] = sum1[n] + grad_now * moment[n]
        return state, moment, sum0, sum1

    def backward(k, carry):
        back, ramp = (list(part) for part in carry)
        grad_now = grad[rows((length - 1 - k) * SUBS, SUBS), :]
        for n in range(modes):
            ramp[n] = factor[n] * (ramp[n] + back[n])
            back[n] = factor[n] * back[n] + grad_now
        return back, ramp

    state, moment, sum0, sum1 = lax.fori_loop(
        0, length, forward, (zero, zero, zero, zero), unroll=UNROLL
    )
    back, ramp = lax.fori_loop(0, length, backward, (zero, zero), unroll=UNROLL)
    height = SENT * modes
    for kind, part in enumerate((state, moment, back, ramp, sum0, sum1)):
        for n in range(modes):
            sent[pl.ds(kind * modes + n, SUBS, stride=height), :] = part[n]


def joined(blocks, decay, span):
    factor = jnp.exp(-decay)
    fading = jnp.exp(-decay * span)
    zero = jnp.zeros_like(decay)
    carry, ramp, total0, total1 = zero, zero, zero, zero
    carries = []
    for state, moment, back, back_ramp, sum0, sum1 in reversed(blocks):
        carries.append(carry)
        near = factor * carry
        total0 = total0 + (sum0 + state * near)
        total1 = total1 + (sum1 + moment * near + state * (factor * ramp + near))
        ramp = fading * (ramp + span * carry) + back_ramp
        carry = fading * carry + back
    all_state, all_moment = zero, zero
    for state, moment, *_ in blocks:
        all_moment = fading * (all_moment + span * all_state) + moment
        all_state = fading * all_state + state
    return carries[::-1], (all_state, all_moment, carry, ramp, total0, total1)


def near_kernel(span, modes, place, decay, data, totals, carries):
    height = SENT * modes
    first = place[0] * WIDE
    for tile in range(SUBS):
        part = lambda b, k: data[b, tile * height + k * modes : tile * height + (k + 1) * modes, :]
        here = decay[:, pl.ds(pl.multiple_of(first + tile * LANES, LANES), LANES)]
        blocks = [[part(b, k) for k in range(SENT)] for b in range(data.shape[0])]
        before, total = joined(blocks, here, span)
        for b, carry in enumerate(before):
            carries[b, tile * modes : (tile + 1) * modes, :] = carry
        for k in range(SENT):
            totals[tile, k * modes : (k + 1) * modes, :] = total[k]


def far_kernel(span, modes, place, decay, data, carries, sums):
    here = decay[:, pl.ds(pl.multiple_of(place[1] * LANES, LANES), LANES)]
    blocks = [
        [data[b, k * modes : (k + 1) * modes, :] for k in range(SENT)] for b in range(data.shape[0])
    ]
    before, total = joined(blocks, here, span)
    for b, carry in enumerate(before):
        carries[b] = carry
    for d in range(sums.shape[0]):
        sums[d, :modes, :] = total[4]
        sums[d, modes:, :] = total[5]


def sum_kernel(modes, carries, sums, out):
    total = sums[0]
    for d in range(1, sums.shape[0]):
        total = total + sums[d]
    for b in range(out.shape[0]):
        out[b, :modes, :] = carries[b]
        out[b, modes:, :] = total


def spread_kernel(span, modes, place, decay, carries, far, out):
    height = BACK * modes
    first = place[0] * WIDE
    blocks = carries.shape[0]
    for tile in range(SUBS):
        here = decay[:, pl.ds(pl.multiple_of(first + tile * LANES, LANES), LANES)]
        fading = jnp.exp(-here * span)
        arriving = far[tile, :modes, :]
        for b in reversed(range(blocks)):
            start = tile * height
            out[b, start : start + modes, :] = (
                carries[b, tile * modes : (tile + 1) * modes, :] + arriving
            )
            out[b, start + modes : start + height, :] = far[tile, modes:, :]
            arriving = fading * arriving


def final_kernel(length, modes, scale, grad, arrived, decay, residues, input_grad, resid_grad,
                 decay_grad, total_rows, decay_rows, residue_rows):
    height = BACK * modes
    split_columns(lambda c: decay[:, c], decay_rows, modes)
    split_columns(lambda c: residues[:, c], residue_rows, modes)
    factor = [jnp.exp(-decay_rows[n * SUBS : (n + 1) * SUBS, :]) for n in range(modes)]
    weight = [residue_rows[n * SUBS : (n + 1) * SUBS, :] for n in range(modes)]
    start = [arrived[pl.ds(n, SUBS, stride=height), :] for n in range(modes)]

    def backward(k, back):
        at = rows((length - 1 - k) * SUBS, SUBS)
        grad_now = grad[at, :]
        back = [factor[n] * back[n] + grad_now for n in range(modes)]
        terms = [weight[n] * back[n] for n in range(modes)]
        while len(terms) > 1:
            terms = [a + b for a, b in zip(terms[::2], terms[1::2])]
        total_rows[at, :] = terms[0]
        return back

    lax.fori_loop(0, length, backward, start, unroll=UNROLL)
    for s in range(SUBS):
        cols = slice(s * LANES, (s + 1) * LANES)
        input_grad[0, :, cols] = total_rows[pl.ds(s, length, stride=SUBS), :].astype(jnp.bfloat16)
        at = s * height
        resid_grad[:, cols] = arrived[at + modes : at + 2 * modes, :] * scale
        decay_grad[:, cols] = (
            -decay[:, cols] * residues[:, cols] * arrived[at + 2 * modes : at + 3 * modes, :] * scale
        )


def on_device(values, gate_values, cotangent, residues, decay_rates):
    _, length, channels = values.shape
    modes = residues.shape[0]
    peers, rows_of = lax.axis_size("ctx"), lax.axis_size("dp")
    far = peers // NEAR
    wide = channels // WIDE
    assert modes == SUBS and wide == NEAR and far == SUBS and values.shape[0] == 1
    me = lax.axis_index("ctx")
    place = jnp.stack([me % NEAR, (me % NEAR) * SUBS + me // NEAR]).astype(jnp.int32)
    near_groups = [[g * NEAR + k for k in range(NEAR)] for g in range(far)]
    far_groups = [[k * NEAR + g for k in range(far)] for g in range(NEAR)]
    shape = lambda *dims: jax.ShapeDtypeStruct(dims, F32)
    vmem = pl.BlockSpec(memory_space=pltpu.VMEM)
    smem = pl.BlockSpec(memory_space=pltpu.SMEM)

    data = pl.BlockSpec((1, length, WIDE), lambda q: (0, 0, q))
    table = pl.BlockSpec((modes, WIDE), lambda q: (0, q))
    flat = lambda size: pl.BlockSpec((size, LANES), lambda q: (q, 0))
    grad, sent = pl.pallas_call(
        functools.partial(local_kernel, length, modes),
        grid=(wide,),
        in_specs=[data, data, data, table],
        out_specs=[flat(length * SUBS), flat(SUBS * SENT * modes)],
        out_shape=[shape(wide * length * SUBS, LANES), shape(wide * SUBS * SENT * modes, LANES)],
        scratch_shapes=[
            pltpu.VMEM((length * SUBS, LANES), F32),
            pltpu.VMEM((modes * SUBS, LANES), F32),
        ],
        name="local",
    )(values, gate_values, cotangent, decay_rates)

    def exchange(x, axis, groups):
        return lax.all_to_all(x, axis, 0, 0, tiled=True, axis_index_groups=groups)

    near_data = exchange(sent.reshape(NEAR, SUBS * SENT * modes, LANES), "ctx", near_groups)
    totals, near_carries = pl.pallas_call(
        functools.partial(near_kernel, float(length), modes),
        in_specs=[smem, vmem, vmem],
        out_specs=[vmem, vmem],
        out_shape=[shape(far, SENT * modes, LANES), shape(NEAR, SUBS * modes, LANES)],
        name="near",
    )(place, decay_rates, near_data)

    far_data = exchange(totals, "ctx", far_groups)
    far_carries, sums = pl.pallas_call(
        functools.partial(far_kernel, float(length * NEAR), modes),
        in_specs=[smem, vmem, vmem],
        out_specs=[vmem, vmem],
        out_shape=[shape(far, modes, LANES), shape(rows_of, 2 * modes, LANES)],
        name="far",
    )(place, decay_rates, far_data)

    all_sums = exchange(sums, "dp", None)
    far_out = pl.pallas_call(
        functools.partial(sum_kernel, modes),
        in_specs=[vmem, vmem],
        out_specs=vmem,
        out_shape=shape(far, BACK * modes, LANES),
        name="sum",
    )(far_carries, all_sums)

    far_back = exchange(far_out, "ctx", far_groups)
    near_out = pl.pallas_call(
        functools.partial(spread_kernel, float(length), modes),
        in_specs=[smem, vmem, vmem, vmem],
        out_specs=vmem,
        out_shape=shape(NEAR, SUBS * BACK * modes, LANES),
        name="spread",
    )(place, decay_rates, near_carries, far_back)

    arrived = exchange(near_out, "ctx", near_groups)
    scale = 1.0 / math.sqrt(rows_of * length * peers)
    return pl.pallas_call(
        functools.partial(final_kernel, length, modes, scale),
        grid=(wide,),
        in_specs=[flat(length * SUBS), flat(SUBS * BACK * modes), table, table],
        out_specs=[data, table, table],
        out_shape=[
            jax.ShapeDtypeStruct(values.shape, jnp.bfloat16),
            shape(modes, channels),
            shape(modes, channels),
        ],
        scratch_shapes=[
            pltpu.VMEM((length * SUBS, LANES), F32),
            pltpu.VMEM((modes * SUBS, LANES), F32),
            pltpu.VMEM((modes * SUBS, LANES), F32),
        ],
        name="final",
    )(grad, arrived.reshape(-1, LANES), decay_rates, residues)


def solution(mesh):
    return jax.shard_map(
        on_device,
        mesh=mesh,
        in_specs=(P("dp", "ctx", None), P("dp", "ctx", None), P("dp", "ctx", None), P(), P()),
        out_specs=(P("dp", "ctx", None), P(), P()),
        check_vma=False,
    )
```

```python
import functools
import math

import jax
import jax.numpy as jnp
from jax import lax
from jax.experimental import pallas as pl
from jax.experimental.pallas import tpu as pltpu
from jax.sharding import PartitionSpec as P

F32 = jnp.float32
LANES = 128
SUBS = 8
WIDE = LANES * SUBS
NEAR = 4
SENT = 6
BACK = 3
UNROLL = 4


def rows(start, size):
    return pl.ds(pl.multiple_of(start, size), size)


def split_columns(read, scratch, length):
    for s in range(SUBS):
        scratch[pl.ds(s, length, stride=SUBS), :] = read(slice(s * LANES, (s + 1) * LANES))


def local_kernel(length, modes, values, gate, cotangent, decay, grad, sent, value_rows, decay_rows):
    split_columns(lambda c: values[0, :, c].astype(F32), value_rows, length)
    split_columns(
        lambda c: cotangent[0, :, c].astype(F32) * gate[0, :, c].astype(F32), grad, length
    )
    split_columns(lambda c: decay[:, c], decay_rows, modes)
    factor = [jnp.exp(-decay_rows[n * SUBS : (n + 1) * SUBS, :]) for n in range(modes)]
    zero = [jnp.zeros((SUBS, LANES), F32)] * modes

    def forward(t, carry):
        state, moment, sum0, sum1 = (list(part) for part in carry)
        value_now = value_rows[rows(t * SUBS, SUBS), :]
        grad_now = grad[rows(t * SUBS, SUBS), :]
        for n in range(modes):
            moment[n] = factor[n] * (moment[n] + state[n])
            state[n] = factor[n] * state[n] + value_now
            sum0[n] = sum0[n] + grad_now * state[n]
            sum1[n] = sum1[n] + grad_now * moment[n]
        return state, moment, sum0, sum1

    def backward(k, carry):
        back, ramp = (list(part) for part in carry)
        grad_now = grad[rows((length - 1 - k) * SUBS, SUBS), :]
        for n in range(modes):
            ramp[n] = factor[n] * (ramp[n] + back[n])
            back[n] = factor[n] * back[n] + grad_now
        return back, ramp

    state, moment, sum0, sum1 = lax.fori_loop(
        0, length, forward, (zero, zero, zero, zero), unroll=UNROLL
    )
    back, ramp = lax.fori_loop(0, length, backward, (zero, zero), unroll=UNROLL)
    height = SENT * modes
    first = pl.multiple_of(pl.program_id(0) * SUBS * height, SUBS * height)
    for kind, part in enumerate((state, moment, back, ramp, sum0, sum1)):
        for n in range(modes):
            sent[pl.ds(first + kind * modes + n, SUBS, stride=height), :] = part[n]


def joined(blocks, decay, span):
    factor = jnp.exp(-decay)
    fading = jnp.exp(-decay * span)
    zero = jnp.zeros_like(decay)
    carry, ramp, total0, total1 = zero, zero, zero, zero
    carries = []
    for state, moment, back, back_ramp, sum0, sum1 in reversed(blocks):
        carries.append(carry)
        near = factor * carry
        total0 = total0 + (sum0 + state * near)
        total1 = total1 + (sum1 + moment * near + state * (factor * ramp + near))
        ramp = fading * (ramp + span * carry) + back_ramp
        carry = fading * carry + back
    all_state, all_moment = zero, zero
    for state, moment, *_ in blocks:
        all_moment = fading * (all_moment + span * all_state) + moment
        all_state = fading * all_state + state
    return carries[::-1], (all_state, all_moment, carry, ramp, total0, total1)


def near_kernel(span, modes, place, decay, data, totals, carries):
    height = SENT * modes
    first = place[0] * WIDE
    for tile in range(SUBS):
        part = lambda b, k: data[b, tile * height + k * modes : tile * height + (k + 1) * modes, :]
        here = decay[:, pl.ds(pl.multiple_of(first + tile * LANES, LANES), LANES)]
        blocks = [[part(b, k) for k in range(SENT)] for b in range(data.shape[0])]
        before, total = joined(blocks, here, span)
        for b, carry in enumerate(before):
            carries[b, tile * modes : (tile + 1) * modes, :] = carry
        for k in range(SENT):
            totals[tile, k * modes : (k + 1) * modes, :] = total[k]


def far_kernel(span, modes, place, decay, data, carries, sums):
    here = decay[:, pl.ds(pl.multiple_of(place[1] * LANES, LANES), LANES)]
    blocks = [
        [data[b, k * modes : (k + 1) * modes, :] for k in range(SENT)] for b in range(data.shape[0])
    ]
    before, total = joined(blocks, here, span)
    for b, carry in enumerate(before):
        carries[b] = carry
    for d in range(sums.shape[0]):
        sums[d, :modes, :] = total[4]
        sums[d, modes:, :] = total[5]


def sum_kernel(modes, carries, sums, out):
    total = sums[0]
    for d in range(1, sums.shape[0]):
        total = total + sums[d]
    for b in range(out.shape[0]):
        out[b, :modes, :] = carries[b]
        out[b, modes:, :] = total


def spread_kernel(span, modes, place, decay, carries, far, out):
    height = BACK * modes
    first = place[0] * WIDE
    blocks = carries.shape[0]
    for tile in range(SUBS):
        here = decay[:, pl.ds(pl.multiple_of(first + tile * LANES, LANES), LANES)]
        fading = jnp.exp(-here * span)
        arriving = far[tile, :modes, :]
        for b in reversed(range(blocks)):
            start = tile * height
            out[b, start : start + modes, :] = (
                carries[b, tile * modes : (tile + 1) * modes, :] + arriving
            )
            out[b, start + modes : start + height, :] = far[tile, modes:, :]
            arriving = fading * arriving


def inner_kernel(length, modes, grad, decay, residues, total, decay_rows, residue_rows):
    split_columns(lambda c: decay[:, c], decay_rows, modes)
    split_columns(lambda c: residues[:, c], residue_rows, modes)
    factor = [jnp.exp(-decay_rows[n * SUBS : (n + 1) * SUBS, :]) for n in range(modes)]
    weight = [residue_rows[n * SUBS : (n + 1) * SUBS, :] for n in range(modes)]

    def backward(k, back):
        at = rows((length - 1 - k) * SUBS, SUBS)
        grad_now = grad[at, :]
        back = [factor[n] * back[n] + grad_now for n in range(modes)]
        total[at, :] = pairwise([weight[n] * back[n] for n in range(modes)])
        return back

    lax.fori_loop(
        0, length, backward, [jnp.zeros((SUBS, LANES), F32)] * modes, unroll=UNROLL
    )


def pairwise(terms):
    while len(terms) > 1:
        terms = [a + b for a, b in zip(terms[::2], terms[1::2])]
    return terms[0]


def final_kernel(length, modes, scale, inner, arrived, decay, residues, input_grad, resid_grad,
                 decay_grad, total_rows, decay_rows, residue_rows):
    height = BACK * modes
    first = pl.multiple_of(pl.program_id(0) * SUBS * height, SUBS * height)
    split_columns(lambda c: decay[:, c], decay_rows, modes)
    split_columns(lambda c: residues[:, c], residue_rows, modes)
    factor = [jnp.exp(-decay_rows[n * SUBS : (n + 1) * SUBS, :]) for n in range(modes)]
    start = [
        residue_rows[n * SUBS : (n + 1) * SUBS, :]
        * arrived[pl.ds(first + n, SUBS, stride=height), :]
        for n in range(modes)
    ]

    def backward(k, tail):
        at = rows((length - 1 - k) * SUBS, SUBS)
        tail = [factor[n] * tail[n] for n in range(modes)]
        total_rows[at, :] = inner[at, :] + pairwise(tail)
        return tail

    lax.fori_loop(0, length, backward, start, unroll=UNROLL)
    for s in range(SUBS):
        cols = slice(s * LANES, (s + 1) * LANES)
        input_grad[0, :, cols] = total_rows[pl.ds(s, length, stride=SUBS), :].astype(jnp.bfloat16)
        at = first + s * height
        resid_grad[:, cols] = arrived[rows(at + modes, modes), :] * scale
        decay_grad[:, cols] = (
            -decay[:, cols] * residues[:, cols] * arrived[rows(at + 2 * modes, modes), :] * scale
        )


def on_device(values, gate_values, cotangent, residues, decay_rates):
    _, length, channels = values.shape
    modes = residues.shape[0]
    peers, rows_of = lax.axis_size("ctx"), lax.axis_size("dp")
    far = peers // NEAR
    wide = channels // WIDE
    assert modes == SUBS and wide == NEAR and far == SUBS and values.shape[0] == 1
    me = lax.axis_index("ctx")
    place = jnp.stack([me % NEAR, (me % NEAR) * SUBS + me // NEAR]).astype(jnp.int32)
    near_groups = [[g * NEAR + k for k in range(NEAR)] for g in range(far)]
    far_groups = [[k * NEAR + g for k in range(far)] for g in range(NEAR)]
    shape = lambda *dims: jax.ShapeDtypeStruct(dims, F32)
    vmem = pl.BlockSpec(memory_space=pltpu.VMEM)
    smem = pl.BlockSpec(memory_space=pltpu.SMEM)
    on_chip = lambda x: pltpu.with_memory_space_constraint(x, pltpu.VMEM)
    held = lambda *dims: pltpu.VMEM(dims, F32)

    near_decay = on_chip(decay_rates)
    data = pl.BlockSpec((1, length, WIDE), lambda q: (0, 0, q))
    table = pl.BlockSpec((modes, WIDE), lambda q: (0, q))
    flat = lambda size: pl.BlockSpec((size, LANES), lambda q: (q, 0))
    grad, sent = pl.pallas_call(
        functools.partial(local_kernel, length, modes),
        grid=(wide,),
        in_specs=[data, data, data, table],
        out_specs=[flat(length * SUBS), vmem],
        out_shape=[shape(wide * length * SUBS, LANES), held(wide * SUBS * SENT * modes, LANES)],
        scratch_shapes=[
            pltpu.VMEM((length * SUBS, LANES), F32),
            pltpu.VMEM((modes * SUBS, LANES), F32),
        ],
        name="local",
    )(values, gate_values, cotangent, decay_rates)

    def exchange(x, axis, groups):
        return lax.all_to_all(x, axis, 0, 0, tiled=True, axis_index_groups=groups)

    near_data = exchange(sent.reshape(NEAR, SUBS * SENT * modes, LANES), "ctx", near_groups)
    inner = pl.pallas_call(
        functools.partial(inner_kernel, length, modes),
        grid=(wide,),
        in_specs=[flat(length * SUBS), table, table],
        out_specs=flat(length * SUBS),
        out_shape=shape(wide * length * SUBS, LANES),
        scratch_shapes=[
            pltpu.VMEM((modes * SUBS, LANES), F32),
            pltpu.VMEM((modes * SUBS, LANES), F32),
        ],
        cost_estimate=pl.CostEstimate(
            flops=4 * modes * length * channels,
            bytes_accessed=8 * length * channels,
            transcendentals=0,
        ),
        name="inner",
    )(grad, decay_rates, residues)
    totals, near_carries = pl.pallas_call(
        functools.partial(near_kernel, float(length), modes),
        in_specs=[smem, vmem, vmem],
        out_specs=[vmem, vmem],
        out_shape=[held(far, SENT * modes, LANES), held(NEAR, SUBS * modes, LANES)],
        name="near",
    )(place, near_decay, on_chip(near_data))

    far_data = exchange(totals, "ctx", far_groups)
    far_carries, sums = pl.pallas_call(
        functools.partial(far_kernel, float(length * NEAR), modes),
        in_specs=[smem, vmem, vmem],
        out_specs=[vmem, vmem],
        out_shape=[held(far, modes, LANES), held(rows_of, 2 * modes, LANES)],
        name="far",
    )(place, near_decay, on_chip(far_data))

    all_sums = exchange(sums, "dp", None)
    far_out = pl.pallas_call(
        functools.partial(sum_kernel, modes),
        in_specs=[vmem, vmem],
        out_specs=vmem,
        out_shape=held(far, BACK * modes, LANES),
        name="sum",
    )(on_chip(far_carries), on_chip(all_sums))

    far_back = exchange(far_out, "ctx", far_groups)
    near_out = pl.pallas_call(
        functools.partial(spread_kernel, float(length), modes),
        in_specs=[smem, vmem, vmem, vmem],
        out_specs=vmem,
        out_shape=held(NEAR, SUBS * BACK * modes, LANES),
        name="spread",
    )(place, near_decay, on_chip(near_carries), on_chip(far_back))

    arrived = exchange(near_out, "ctx", near_groups)
    scale = 1.0 / math.sqrt(rows_of * length * peers)
    return pl.pallas_call(
        functools.partial(final_kernel, length, modes, scale),
        grid=(wide,),
        in_specs=[flat(length * SUBS), vmem, table, table],
        out_specs=[data, table, table],
        out_shape=[
            jax.ShapeDtypeStruct(values.shape, jnp.bfloat16),
            shape(modes, channels),
            shape(modes, channels),
        ],
        scratch_shapes=[
            pltpu.VMEM((length * SUBS, LANES), F32),
            pltpu.VMEM((modes * SUBS, LANES), F32),
            pltpu.VMEM((modes * SUBS, LANES), F32),
        ],
        name="final",
    )(inner, on_chip(arrived.reshape(-1, LANES)), decay_rates, residues)


def solution(mesh):
    return jax.shard_map(
        on_device,
        mesh=mesh,
        in_specs=(P("dp", "ctx", None), P("dp", "ctx", None), P("dp", "ctx", None), P(), P()),
        out_specs=(P("dp", "ctx", None), P(), P()),
        check_vma=False,
    )
```

```python
import functools
import math

import jax
import jax.numpy as jnp
from jax import lax
from jax.experimental import pallas as pl
from jax.experimental.pallas import tpu as pltpu
from jax.sharding import PartitionSpec as P

F32 = jnp.float32
LANES = 128
SUBS = 8
WIDE = LANES * SUBS
NEAR = 4
SENT = 6
BACK = 3
UNROLL = 4
TILES = 4


def rows(start, size):
    return pl.ds(pl.multiple_of(start, size), size)


def split_columns(read, scratch, length):
    for s in range(SUBS):
        scratch[pl.ds(s, length, stride=SUBS), :] = read(slice(s * LANES, (s + 1) * LANES))


def spread_row(ref, row):
    return ref[pl.ds(row, SUBS, stride=0), :]


def spread_cell(ref, row, columns):
    return jnp.broadcast_to(ref[row : row + 1, columns], (SUBS, LANES))


def local_kernel(length, modes, values, gate, cotangent, decay, grad, sent, value_rows, grad_rows):
    height = SENT * modes
    step = pl.program_id(0)
    for s in range(SUBS):
        c, at = slice(s * LANES, (s + 1) * LANES), slice(s * length, (s + 1) * length)
        value_rows[at, :] = values[0, :, c].astype(F32)
        product = cotangent[0, :, c].astype(F32) * gate[0, :, c].astype(F32)
        grad_rows[at, :] = product
        grad[:, c] = product
    zero = jnp.zeros((modes, LANES), F32)
    for begin in range(0, SUBS, TILES):
        columns = [slice((begin + i) * LANES, (begin + i + 1) * LANES) for i in range(TILES)]
        factor = [jnp.exp(-decay[:, c]) for c in columns]

        def advance(chunk, carry):
            carry = [list(part) for part in carry]
            early = pl.multiple_of(chunk * SUBS, SUBS)
            late = pl.multiple_of(length - SUBS - chunk * SUBS, SUBS)
            for j in range(SUBS):
                for i in range(TILES):
                    first = (begin + i) * length
                    state, moment, back, ramp, sum0, sum1 = carry[i]
                    value_now = spread_row(value_rows, first + early + j)
                    grad_now = spread_row(grad_rows, first + early + j)
                    moment = factor[i] * (moment + state)
                    state = factor[i] * state + value_now
                    sum0 = sum0 + grad_now * state
                    sum1 = sum1 + grad_now * moment
                    ramp = factor[i] * (ramp + back)
                    back = factor[i] * back + spread_row(
                        grad_rows, first + late + SUBS - 1 - j
                    )
                    carry[i] = [state, moment, back, ramp, sum0, sum1]
            return carry

        carry = lax.fori_loop(0, length // SUBS, advance, [[zero] * SENT for _ in columns])
        for i, parts in enumerate(carry):
            for kind, part in enumerate(parts):
                at = (step * SUBS + begin + i) * height + kind * modes
                sent[rows(at, modes), :] = part


def joined(blocks, decay, span):
    factor = jnp.exp(-decay)
    fading = jnp.exp(-decay * span)
    zero = jnp.zeros_like(decay)
    carry, ramp, total0, total1 = zero, zero, zero, zero
    carries = []
    for state, moment, back, back_ramp, sum0, sum1 in reversed(blocks):
        carries.append(carry)
        near = factor * carry
        total0 = total0 + (sum0 + state * near)
        total1 = total1 + (sum1 + moment * near + state * (factor * ramp + near))
        ramp = fading * (ramp + span * carry) + back_ramp
        carry = fading * carry + back
    all_state, all_moment = zero, zero
    for state, moment, *_ in blocks:
        all_moment = fading * (all_moment + span * all_state) + moment
        all_state = fading * all_state + state
    return carries[::-1], (all_state, all_moment, carry, ramp, total0, total1)


def near_kernel(span, modes, place, decay, data, totals, carries):
    height = SENT * modes
    first = place[0] * WIDE
    for tile in range(SUBS):
        part = lambda b, k: data[b, tile * height + k * modes : tile * height + (k + 1) * modes, :]
        here = decay[:, pl.ds(pl.multiple_of(first + tile * LANES, LANES), LANES)]
        blocks = [[part(b, k) for k in range(SENT)] for b in range(data.shape[0])]
        before, total = joined(blocks, here, span)
        for b, carry in enumerate(before):
            carries[b, tile * modes : (tile + 1) * modes, :] = carry
        for k in range(SENT):
            totals[tile, k * modes : (k + 1) * modes, :] = total[k]


def far_kernel(span, modes, place, decay, data, carries, sums):
    here = decay[:, pl.ds(pl.multiple_of(place[1] * LANES, LANES), LANES)]
    blocks = [
        [data[b, k * modes : (k + 1) * modes, :] for k in range(SENT)] for b in range(data.shape[0])
    ]
    before, total = joined(blocks, here, span)
    for b, carry in enumerate(before):
        carries[b] = carry
    for d in range(sums.shape[0]):
        sums[d, :modes, :] = total[4]
        sums[d, modes:, :] = total[5]


def sum_kernel(modes, carries, sums, out):
    total = sums[0]
    for d in range(1, sums.shape[0]):
        total = total + sums[d]
    for b in range(out.shape[0]):
        out[b, :modes, :] = carries[b]
        out[b, modes:, :] = total


def spread_kernel(span, modes, place, decay, carries, far, out):
    height = BACK * modes
    first = place[0] * WIDE
    blocks = carries.shape[0]
    for tile in range(SUBS):
        here = decay[:, pl.ds(pl.multiple_of(first + tile * LANES, LANES), LANES)]
        fading = jnp.exp(-here * span)
        arriving = far[tile, :modes, :]
        for b in reversed(range(blocks)):
            start = tile * height
            out[b, start : start + modes, :] = (
                carries[b, tile * modes : (tile + 1) * modes, :] + arriving
            )
            out[b, start + modes : start + height, :] = far[tile, modes:, :]
            arriving = fading * arriving


def pairwise(terms):
    while len(terms) > 1:
        terms = [a + b for a, b in zip(terms[::2], terms[1::2])]
    return terms[0]


def inner_kernel(length, modes, grad, decay, residues, inner, grad_rows, total_rows, decay_rows,
                 residue_rows):
    step = pl.program_id(0)
    split_columns(lambda c: grad[:, c], grad_rows, length)
    split_columns(lambda c: decay[:, c], decay_rows, modes)
    split_columns(lambda c: residues[:, c], residue_rows, modes)
    factor = [jnp.exp(-decay_rows[n * SUBS : (n + 1) * SUBS, :]) for n in range(modes)]
    weight = [residue_rows[n * SUBS : (n + 1) * SUBS, :] for n in range(modes)]

    def backward(k, back):
        at = rows((length - 1 - k) * SUBS, SUBS)
        grad_now = grad_rows[at, :]
        back = [factor[n] * back[n] + grad_now for n in range(modes)]
        total_rows[at, :] = pairwise([weight[n] * back[n] for n in range(modes)])
        return back

    lax.fori_loop(
        0, length, backward, [jnp.zeros((SUBS, LANES), F32)] * modes, unroll=UNROLL
    )
    for s in range(SUBS):
        to_inner = pl.ds(pl.multiple_of(step * WIDE + s * LANES, LANES), LANES)
        inner[:, to_inner] = total_rows[pl.ds(s, length, stride=SUBS), :]


def final_kernel(length, modes, scale, inner, arrived, decay, residues, input_grad, resid_grad,
                 decay_grad):
    height = BACK * modes
    step = pl.program_id(0)
    remaining = (
        SUBS - lax.broadcasted_iota(jnp.int32, (SUBS, LANES), 0)
    ).astype(F32)
    for s in range(SUBS):
        c = slice(s * LANES, (s + 1) * LANES)
        from_inner = pl.ds(pl.multiple_of(step * WIDE + s * LANES, LANES), LANES)
        at = (step * SUBS + s) * height
        tail, chunk_factor = [], []
        for n in range(modes):
            rate = spread_cell(decay, n, c)
            carry = spread_row(arrived, at + n)
            tail.append(spread_cell(residues, n, c) * carry * jnp.exp(-rate * remaining))
            chunk_factor.append(jnp.exp(-rate * float(SUBS)))
        for low in range(length - 2 * SUBS, -1, -2 * SUBS):
            pair = []
            for begin in (low + SUBS, low):
                pair.append(inner[begin : begin + SUBS, from_inner] + pairwise(tail))
                tail = [f * z for f, z in zip(chunk_factor, tail)]
            input_grad[0, low : low + 2 * SUBS, c] = jnp.concatenate(pair[::-1], 0).astype(
                jnp.bfloat16
            )
        resid_grad[:, c] = arrived[rows(at + modes, modes), :] * scale
        decay_grad[:, c] = (
            -decay[:, c] * residues[:, c] * arrived[rows(at + 2 * modes, modes), :] * scale
        )


def on_device(values, gate_values, cotangent, residues, decay_rates):
    _, length, channels = values.shape
    modes = residues.shape[0]
    peers, rows_of = lax.axis_size("ctx"), lax.axis_size("dp")
    far = peers // NEAR
    wide = channels // WIDE
    assert modes == SUBS and wide == NEAR and far == SUBS and values.shape[0] == 1
    me = lax.axis_index("ctx")
    place = jnp.stack([me % NEAR, (me % NEAR) * SUBS + me // NEAR]).astype(jnp.int32)
    near_groups = [[g * NEAR + k for k in range(NEAR)] for g in range(far)]
    far_groups = [[k * NEAR + g for k in range(far)] for g in range(NEAR)]
    shape = lambda *dims: jax.ShapeDtypeStruct(dims, F32)
    vmem = pl.BlockSpec(memory_space=pltpu.VMEM)
    smem = pl.BlockSpec(memory_space=pltpu.SMEM)
    on_chip = lambda x: pltpu.with_memory_space_constraint(x, pltpu.VMEM)
    held = lambda *dims: pltpu.VMEM(dims, F32)

    small = pltpu.CompilerParams(vmem_limit_bytes=16 << 20)
    near_decay = on_chip(decay_rates)
    data = pl.BlockSpec((1, length, WIDE), lambda q: (0, 0, q))
    block = pl.BlockSpec((length, WIDE), lambda q: (0, q))
    table = pl.BlockSpec((modes, WIDE), lambda q: (0, q))
    grad, sent = pl.pallas_call(
        functools.partial(local_kernel, length, modes),
        grid=(wide,),
        in_specs=[data, data, data, table],
        out_specs=[block, vmem],
        out_shape=[shape(length, channels), held(wide * SUBS * SENT * modes, LANES)],
        scratch_shapes=[pltpu.VMEM((SUBS * length, LANES), F32)] * 2,
        name="local",
    )(values, gate_values, cotangent, decay_rates)

    def exchange(x, axis, groups):
        return lax.all_to_all(x, axis, 0, 0, tiled=True, axis_index_groups=groups)

    near_data = exchange(sent.reshape(NEAR, SUBS * SENT * modes, LANES), "ctx", near_groups)
    inner = pl.pallas_call(
        functools.partial(inner_kernel, length, modes),
        grid=(wide,),
        in_specs=[block, table, table],
        out_specs=vmem,
        out_shape=held(length, channels),
        scratch_shapes=[pltpu.VMEM((length * SUBS, LANES), F32)] * 2
        + [pltpu.VMEM((modes * SUBS, LANES), F32)] * 2,
        cost_estimate=pl.CostEstimate(
            flops=4 * modes * length * channels,
            bytes_accessed=8 * length * channels,
            transcendentals=0,
        ),
        compiler_params=pltpu.CompilerParams(vmem_limit_bytes=60 << 20),
        name="inner",
    )(grad, decay_rates, residues)
    totals, near_carries = pl.pallas_call(
        functools.partial(near_kernel, float(length), modes),
        in_specs=[smem, vmem, vmem],
        out_specs=[vmem, vmem],
        out_shape=[held(far, SENT * modes, LANES), held(NEAR, SUBS * modes, LANES)],
        name="near",
    )(place, near_decay, on_chip(near_data))

    far_data = exchange(totals, "ctx", far_groups)
    far_carries, sums = pl.pallas_call(
        functools.partial(far_kernel, float(length * NEAR), modes),
        in_specs=[smem, vmem, vmem],
        out_specs=[vmem, vmem],
        out_shape=[held(far, modes, LANES), held(rows_of, 2 * modes, LANES)],
        name="far",
    )(place, near_decay, on_chip(far_data))

    all_sums = exchange(sums, "dp", None)
    far_out = pl.pallas_call(
        functools.partial(sum_kernel, modes),
        in_specs=[vmem, vmem],
        out_specs=vmem,
        out_shape=held(far, BACK * modes, LANES),
        name="sum",
    )(on_chip(far_carries), on_chip(all_sums))

    far_back = exchange(far_out, "ctx", far_groups)
    near_out = pl.pallas_call(
        functools.partial(spread_kernel, float(length), modes),
        in_specs=[smem, vmem, vmem, vmem],
        out_specs=vmem,
        out_shape=held(NEAR, SUBS * BACK * modes, LANES),
        name="spread",
    )(place, near_decay, on_chip(near_carries), on_chip(far_back))

    arrived = exchange(near_out, "ctx", near_groups)
    scale = 1.0 / math.sqrt(rows_of * length * peers)
    return pl.pallas_call(
        functools.partial(final_kernel, length, modes, scale),
        grid=(wide,),
        in_specs=[vmem, vmem, table, table],
        out_specs=[data, table, table],
        out_shape=[
            jax.ShapeDtypeStruct(values.shape, jnp.bfloat16),
            shape(modes, channels),
            shape(modes, channels),
        ],
        compiler_params=small,
        name="final",
    )(on_chip(inner), on_chip(arrived.reshape(-1, LANES)), decay_rates, residues)


def solution(mesh):
    return jax.shard_map(
        on_device,
        mesh=mesh,
        in_specs=(P("dp", "ctx", None), P("dp", "ctx", None), P("dp", "ctx", None), P(), P()),
        out_specs=(P("dp", "ctx", None), P(), P()),
        check_vma=False,
    )
```

```python
import functools
import math

import jax
import jax.numpy as jnp
from jax import lax
from jax.experimental import pallas as pl
from jax.experimental.pallas import tpu as pltpu
from jax.sharding import PartitionSpec as P

F32 = jnp.float32
LANES = 128
SUBS = 8
WIDE = LANES * SUBS
NEAR = 4
SENT = 6
BACK = 3
UNROLL = 4
TILES = 4


def rows(start, size):
    return pl.ds(pl.multiple_of(start, size), size)


def split_columns(read, scratch, length):
    for s in range(SUBS):
        scratch[pl.ds(s, length, stride=SUBS), :] = read(slice(s * LANES, (s + 1) * LANES))


def spread_row(ref, row):
    return ref[pl.ds(row, SUBS, stride=0), :]


def spread_cell(ref, row, columns):
    return jnp.broadcast_to(ref[row : row + 1, columns], (SUBS, LANES))


def local_kernel(length, modes, values, gate, cotangent, decay, sent, value_rows, grad_rows):
    height = SENT * modes
    step = pl.program_id(0)
    for s in range(SUBS):
        c, at = slice(s * LANES, (s + 1) * LANES), slice(s * length, (s + 1) * length)
        value_rows[at, :] = values[0, :, c].astype(F32)
        grad_rows[at, :] = cotangent[0, :, c].astype(F32) * gate[0, :, c].astype(F32)
    zero = jnp.zeros((modes, LANES), F32)
    for begin in range(0, SUBS, TILES):
        columns = [slice((begin + i) * LANES, (begin + i + 1) * LANES) for i in range(TILES)]
        factor = [jnp.exp(-decay[:, c]) for c in columns]

        def advance(chunk, carry):
            carry = [list(part) for part in carry]
            early = pl.multiple_of(chunk * SUBS, SUBS)
            late = pl.multiple_of(length - SUBS - chunk * SUBS, SUBS)
            for j in range(SUBS):
                for i in range(TILES):
                    first = (begin + i) * length
                    state, moment, back, ramp, sum0, sum1 = carry[i]
                    value_now = spread_row(value_rows, first + early + j)
                    grad_now = spread_row(grad_rows, first + early + j)
                    moment = factor[i] * (moment + state)
                    state = factor[i] * state + value_now
                    sum0 = sum0 + grad_now * state
                    sum1 = sum1 + grad_now * moment
                    ramp = factor[i] * (ramp + back)
                    back = factor[i] * back + spread_row(
                        grad_rows, first + late + SUBS - 1 - j
                    )
                    carry[i] = [state, moment, back, ramp, sum0, sum1]
            return carry

        carry = lax.fori_loop(0, length // SUBS, advance, [[zero] * SENT for _ in columns])
        for i, parts in enumerate(carry):
            for kind, part in enumerate(parts):
                at = (step * SUBS + begin + i) * height + kind * modes
                sent[rows(at, modes), :] = part


def joined(blocks, decay, span):
    factor = jnp.exp(-decay)
    fading = jnp.exp(-decay * span)
    zero = jnp.zeros_like(decay)
    carry, ramp, total0, total1 = zero, zero, zero, zero
    carries = []
    for state, moment, back, back_ramp, sum0, sum1 in reversed(blocks):
        carries.append(carry)
        near = factor * carry
        total0 = total0 + (sum0 + state * near)
        total1 = total1 + (sum1 + moment * near + state * (factor * ramp + near))
        ramp = fading * (ramp + span * carry) + back_ramp
        carry = fading * carry + back
    all_state, all_moment = zero, zero
    for state, moment, *_ in blocks:
        all_moment = fading * (all_moment + span * all_state) + moment
        all_state = fading * all_state + state
    return carries[::-1], (all_state, all_moment, carry, ramp, total0, total1)


def near_kernel(span, modes, place, decay, data, totals, carries):
    height = SENT * modes
    first = place[0] * WIDE
    for tile in range(SUBS):
        part = lambda b, k: data[b, tile * height + k * modes : tile * height + (k + 1) * modes, :]
        here = decay[:, pl.ds(pl.multiple_of(first + tile * LANES, LANES), LANES)]
        blocks = [[part(b, k) for k in range(SENT)] for b in range(data.shape[0])]
        before, total = joined(blocks, here, span)
        for b, carry in enumerate(before):
            carries[b, tile * modes : (tile + 1) * modes, :] = carry
        for k in range(SENT):
            totals[tile, k * modes : (k + 1) * modes, :] = total[k]


def far_kernel(span, modes, place, decay, data, carries, sums):
    here = decay[:, pl.ds(pl.multiple_of(place[1] * LANES, LANES), LANES)]
    blocks = [
        [data[b, k * modes : (k + 1) * modes, :] for k in range(SENT)] for b in range(data.shape[0])
    ]
    before, total = joined(blocks, here, span)
    for b, carry in enumerate(before):
        carries[b] = carry
    for d in range(sums.shape[0]):
        sums[d, :modes, :] = total[4]
        sums[d, modes:, :] = total[5]


def sum_kernel(modes, carries, sums, out):
    total = sums[0]
    for d in range(1, sums.shape[0]):
        total = total + sums[d]
    for b in range(out.shape[0]):
        out[b, :modes, :] = carries[b]
        out[b, modes:, :] = total


def spread_kernel(span, modes, place, decay, carries, far, out):
    height = BACK * modes
    first = place[0] * WIDE
    blocks = carries.shape[0]
    for tile in range(SUBS):
        here = decay[:, pl.ds(pl.multiple_of(first + tile * LANES, LANES), LANES)]
        fading = jnp.exp(-here * span)
        arriving = far[tile, :modes, :]
        for b in reversed(range(blocks)):
            start = tile * height
            out[b, start : start + modes, :] = (
                carries[b, tile * modes : (tile + 1) * modes, :] + arriving
            )
            out[b, start + modes : start + height, :] = far[tile, modes:, :]
            arriving = fading * arriving


def pairwise(terms):
    while len(terms) > 1:
        terms = [a + b for a, b in zip(terms[::2], terms[1::2])]
    return terms[0]


def inner_kernel(length, modes, gate, cotangent, decay, residues, inner, grad_rows, total_rows,
                 decay_rows, residue_rows):
    step = pl.program_id(0)
    split_columns(
        lambda c: cotangent[0, :, c].astype(F32) * gate[0, :, c].astype(F32), grad_rows, length
    )
    split_columns(lambda c: decay[:, c], decay_rows, modes)
    split_columns(lambda c: residues[:, c], residue_rows, modes)
    factor = [jnp.exp(-decay_rows[n * SUBS : (n + 1) * SUBS, :]) for n in range(modes)]
    weight = [residue_rows[n * SUBS : (n + 1) * SUBS, :] for n in range(modes)]

    def backward(k, back):
        at = rows((length - 1 - k) * SUBS, SUBS)
        grad_now = grad_rows[at, :]
        back = [factor[n] * back[n] + grad_now for n in range(modes)]
        total_rows[at, :] = pairwise([weight[n] * back[n] for n in range(modes)])
        return back

    lax.fori_loop(
        0, length, backward, [jnp.zeros((SUBS, LANES), F32)] * modes, unroll=UNROLL
    )
    for s in range(SUBS):
        to_inner = pl.ds(pl.multiple_of(step * WIDE + s * LANES, LANES), LANES)
        inner[:, to_inner] = total_rows[pl.ds(s, length, stride=SUBS), :]


def final_kernel(length, modes, scale, inner, arrived, decay, residues, input_grad, resid_grad,
                 decay_grad):
    height = BACK * modes
    step = pl.program_id(0)
    remaining = (
        SUBS - lax.broadcasted_iota(jnp.int32, (SUBS, LANES), 0)
    ).astype(F32)
    for s in range(SUBS):
        c = slice(s * LANES, (s + 1) * LANES)
        from_inner = pl.ds(pl.multiple_of(step * WIDE + s * LANES, LANES), LANES)
        at = (step * SUBS + s) * height
        tail, chunk_factor = [], []
        for n in range(modes):
            rate = spread_cell(decay, n, c)
            carry = spread_row(arrived, at + n)
            tail.append(spread_cell(residues, n, c) * carry * jnp.exp(-rate * remaining))
            chunk_factor.append(jnp.exp(-rate * float(SUBS)))
        for low in range(length - 2 * SUBS, -1, -2 * SUBS):
            pair = []
            for begin in (low + SUBS, low):
                pair.append(inner[begin : begin + SUBS, from_inner] + pairwise(tail))
                tail = [f * z for f, z in zip(chunk_factor, tail)]
            input_grad[0, low : low + 2 * SUBS, c] = jnp.concatenate(pair[::-1], 0).astype(
                jnp.bfloat16
            )
        resid_grad[:, c] = arrived[rows(at + modes, modes), :] * scale
        decay_grad[:, c] = (
            -decay[:, c] * residues[:, c] * arrived[rows(at + 2 * modes, modes), :] * scale
        )


def on_device(values, gate_values, cotangent, residues, decay_rates):
    _, length, channels = values.shape
    modes = residues.shape[0]
    peers, rows_of = lax.axis_size("ctx"), lax.axis_size("dp")
    far = peers // NEAR
    wide = channels // WIDE
    assert modes == SUBS and wide == NEAR and far == SUBS and values.shape[0] == 1
    me = lax.axis_index("ctx")
    place = jnp.stack([me % NEAR, (me % NEAR) * SUBS + me // NEAR]).astype(jnp.int32)
    place, values = lax.optimization_barrier((place, values))
    near_groups = [[g * NEAR + k for k in range(NEAR)] for g in range(far)]
    far_groups = [[k * NEAR + g for k in range(far)] for g in range(NEAR)]
    shape = lambda *dims: jax.ShapeDtypeStruct(dims, F32)
    vmem = pl.BlockSpec(memory_space=pltpu.VMEM)
    smem = pl.BlockSpec(memory_space=pltpu.SMEM)
    on_chip = lambda x: pltpu.with_memory_space_constraint(x, pltpu.VMEM)
    held = lambda *dims: pltpu.VMEM(dims, F32)

    small = pltpu.CompilerParams(vmem_limit_bytes=16 << 20)
    near_decay = on_chip(decay_rates)
    data = pl.BlockSpec((1, length, WIDE), lambda q: (0, 0, q))
    table = pl.BlockSpec((modes, WIDE), lambda q: (0, q))
    sent = pl.pallas_call(
        functools.partial(local_kernel, length, modes),
        grid=(wide,),
        in_specs=[data, data, data, table],
        out_specs=vmem,
        out_shape=held(wide * SUBS * SENT * modes, LANES),
        scratch_shapes=[pltpu.VMEM((SUBS * length, LANES), F32)] * 2,
        name="local",
    )(values, gate_values, cotangent, decay_rates)

    def exchange(x, axis, groups):
        return lax.all_to_all(x, axis, 0, 0, tiled=True, axis_index_groups=groups)

    near_data = exchange(sent.reshape(NEAR, SUBS * SENT * modes, LANES), "ctx", near_groups)
    inner = pl.pallas_call(
        functools.partial(inner_kernel, length, modes),
        grid=(wide,),
        in_specs=[data, data, table, table],
        out_specs=vmem,
        out_shape=held(length, channels),
        scratch_shapes=[pltpu.VMEM((length * SUBS, LANES), F32)] * 2
        + [pltpu.VMEM((modes * SUBS, LANES), F32)] * 2,
        cost_estimate=pl.CostEstimate(
            flops=4 * modes * length * channels,
            bytes_accessed=8 * length * channels,
            transcendentals=0,
        ),
        compiler_params=pltpu.CompilerParams(vmem_limit_bytes=60 << 20),
        name="inner",
    )(gate_values, cotangent, decay_rates, residues)
    totals, near_carries = pl.pallas_call(
        functools.partial(near_kernel, float(length), modes),
        in_specs=[smem, vmem, vmem],
        out_specs=[vmem, vmem],
        out_shape=[held(far, SENT * modes, LANES), held(NEAR, SUBS * modes, LANES)],
        name="near",
    )(place, near_decay, on_chip(near_data))

    far_data = exchange(totals, "ctx", far_groups)
    far_carries, sums = pl.pallas_call(
        functools.partial(far_kernel, float(length * NEAR), modes),
        in_specs=[smem, vmem, vmem],
        out_specs=[vmem, vmem],
        out_shape=[held(far, modes, LANES), held(rows_of, 2 * modes, LANES)],
        name="far",
    )(place, near_decay, on_chip(far_data))

    all_sums = exchange(sums, "dp", None)
    far_out = pl.pallas_call(
        functools.partial(sum_kernel, modes),
        in_specs=[vmem, vmem],
        out_specs=vmem,
        out_shape=held(far, BACK * modes, LANES),
        name="sum",
    )(on_chip(far_carries), on_chip(all_sums))

    far_back = exchange(far_out, "ctx", far_groups)
    near_out = pl.pallas_call(
        functools.partial(spread_kernel, float(length), modes),
        in_specs=[smem, vmem, vmem, vmem],
        out_specs=vmem,
        out_shape=held(NEAR, SUBS * BACK * modes, LANES),
        name="spread",
    )(place, near_decay, on_chip(near_carries), on_chip(far_back))

    arrived = exchange(near_out, "ctx", near_groups)
    scale = 1.0 / math.sqrt(rows_of * length * peers)
    return pl.pallas_call(
        functools.partial(final_kernel, length, modes, scale),
        grid=(wide,),
        in_specs=[vmem, vmem, table, table],
        out_specs=[data, table, table],
        out_shape=[
            jax.ShapeDtypeStruct(values.shape, jnp.bfloat16),
            shape(modes, channels),
            shape(modes, channels),
        ],
        compiler_params=small,
        name="final",
    )(on_chip(inner), on_chip(arrived.reshape(-1, LANES)), decay_rates, residues)


def solution(mesh):
    return jax.shard_map(
        on_device,
        mesh=mesh,
        in_specs=(P("dp", "ctx", None), P("dp", "ctx", None), P("dp", "ctx", None), P(), P()),
        out_specs=(P("dp", "ctx", None), P(), P()),
        check_vma=False,
    )
```

```python
import functools
import math

import jax
import jax.numpy as jnp
from jax import lax
from jax.experimental import pallas as pl
from jax.experimental.pallas import tpu as pltpu
from jax.sharding import PartitionSpec as P

F32 = jnp.float32
LANES = 128
SUBS = 8
WIDE = LANES * SUBS
NEAR = 4
SENT = 6
BACK = 3
UNROLL = 4
FINAL = 2
TILES = 4


def rows(start, size):
    return pl.ds(pl.multiple_of(start, size), size)


def split_columns(read, scratch, length):
    for s in range(SUBS):
        scratch[pl.ds(s, length, stride=SUBS), :] = read(slice(s * LANES, (s + 1) * LANES))


def spread_row(ref, row):
    return ref[pl.ds(row, SUBS, stride=0), :]


def spread_cell(ref, row, columns):
    return jnp.broadcast_to(ref[row : row + 1, columns], (SUBS, LANES))


def local_kernel(length, modes, values, gate, cotangent, decay, sent, value_rows, grad_rows):
    height = SENT * modes
    step = pl.program_id(0)
    for s in range(SUBS):
        c, at = slice(s * LANES, (s + 1) * LANES), slice(s * length, (s + 1) * length)
        value_rows[at, :] = values[0, :, c].astype(F32)
        grad_rows[at, :] = cotangent[0, :, c].astype(F32) * gate[0, :, c].astype(F32)
    zero = jnp.zeros((modes, LANES), F32)
    for begin in range(0, SUBS, TILES):
        columns = [slice((begin + i) * LANES, (begin + i + 1) * LANES) for i in range(TILES)]
        factor = [jnp.exp(-decay[:, c]) for c in columns]

        def advance(chunk, carry):
            carry = [list(part) for part in carry]
            early = pl.multiple_of(chunk * SUBS, SUBS)
            late = pl.multiple_of(length - SUBS - chunk * SUBS, SUBS)
            for j in range(SUBS):
                for i in range(TILES):
                    first = (begin + i) * length
                    state, moment, back, ramp, sum0, sum1 = carry[i]
                    value_now = spread_row(value_rows, first + early + j)
                    grad_now = spread_row(grad_rows, first + early + j)
                    moment = factor[i] * (moment + state)
                    state = factor[i] * state + value_now
                    sum0 = sum0 + grad_now * state
                    sum1 = sum1 + grad_now * moment
                    ramp = factor[i] * (ramp + back)
                    back = factor[i] * back + spread_row(
                        grad_rows, first + late + SUBS - 1 - j
                    )
                    carry[i] = [state, moment, back, ramp, sum0, sum1]
            return carry

        carry = lax.fori_loop(0, length // SUBS, advance, [[zero] * SENT for _ in columns])
        for i, parts in enumerate(carry):
            for kind, part in enumerate(parts):
                at = (step * SUBS + begin + i) * height + kind * modes
                sent[rows(at, modes), :] = part


def joined(blocks, decay, span):
    factor = jnp.exp(-decay)
    fading = jnp.exp(-decay * span)
    zero = jnp.zeros_like(decay)
    carry, ramp, total0, total1 = zero, zero, zero, zero
    carries = []
    for state, moment, back, back_ramp, sum0, sum1 in reversed(blocks):
        carries.append(carry)
        near = factor * carry
        total0 = total0 + (sum0 + state * near)
        total1 = total1 + (sum1 + moment * near + state * (factor * ramp + near))
        ramp = fading * (ramp + span * carry) + back_ramp
        carry = fading * carry + back
    all_state, all_moment = zero, zero
    for state, moment, *_ in blocks:
        all_moment = fading * (all_moment + span * all_state) + moment
        all_state = fading * all_state + state
    return carries[::-1], (all_state, all_moment, carry, ramp, total0, total1)


def near_kernel(span, modes, place, decay, data, totals, carries):
    height = SENT * modes
    first = place[0] * WIDE
    for tile in range(SUBS):
        part = lambda b, k: data[b, tile * height + k * modes : tile * height + (k + 1) * modes, :]
        here = decay[:, pl.ds(pl.multiple_of(first + tile * LANES, LANES), LANES)]
        blocks = [[part(b, k) for k in range(SENT)] for b in range(data.shape[0])]
        before, total = joined(blocks, here, span)
        for b, carry in enumerate(before):
            carries[b, tile * modes : (tile + 1) * modes, :] = carry
        for k in range(SENT):
            totals[tile, k * modes : (k + 1) * modes, :] = total[k]


def far_kernel(span, modes, place, decay, data, carries, sums):
    here = decay[:, pl.ds(pl.multiple_of(place[1] * LANES, LANES), LANES)]
    blocks = [
        [data[b, k * modes : (k + 1) * modes, :] for k in range(SENT)] for b in range(data.shape[0])
    ]
    before, total = joined(blocks, here, span)
    for b, carry in enumerate(before):
        carries[b] = carry
    for d in range(sums.shape[0]):
        sums[d, :modes, :] = total[4]
        sums[d, modes:, :] = total[5]


def sum_kernel(modes, carries, sums, out):
    total = sums[0]
    for d in range(1, sums.shape[0]):
        total = total + sums[d]
    for b in range(out.shape[0]):
        out[b, :modes, :] = carries[b]
        out[b, modes:, :] = total


def spread_kernel(span, modes, place, decay, carries, far, out):
    height = BACK * modes
    first = place[0] * WIDE
    blocks = carries.shape[0]
    for tile in range(SUBS):
        here = decay[:, pl.ds(pl.multiple_of(first + tile * LANES, LANES), LANES)]
        fading = jnp.exp(-here * span)
        arriving = far[tile, :modes, :]
        for b in reversed(range(blocks)):
            start = tile * height
            out[b, start : start + modes, :] = (
                carries[b, tile * modes : (tile + 1) * modes, :] + arriving
            )
            out[b, start + modes : start + height, :] = far[tile, modes:, :]
            arriving = fading * arriving


def pairwise(terms):
    while len(terms) > 1:
        terms = [a + b for a, b in zip(terms[::2], terms[1::2])]
    return terms[0]


def inner_kernel(length, modes, gate, cotangent, decay, residues, inner, grad_rows, total_rows,
                 decay_rows, residue_rows):
    step = pl.program_id(0)
    split_columns(
        lambda c: cotangent[0, :, c].astype(F32) * gate[0, :, c].astype(F32), grad_rows, length
    )
    split_columns(lambda c: decay[:, c], decay_rows, modes)
    split_columns(lambda c: residues[:, c], residue_rows, modes)
    factor = [jnp.exp(-decay_rows[n * SUBS : (n + 1) * SUBS, :]) for n in range(modes)]
    weight = [residue_rows[n * SUBS : (n + 1) * SUBS, :] for n in range(modes)]

    def backward(k, back):
        at = rows((length - 1 - k) * SUBS, SUBS)
        grad_now = grad_rows[at, :]
        back = [factor[n] * back[n] + grad_now for n in range(modes)]
        total_rows[at, :] = pairwise([weight[n] * back[n] for n in range(modes)])
        return back

    lax.fori_loop(
        0, length, backward, [jnp.zeros((SUBS, LANES), F32)] * modes, unroll=UNROLL
    )
    for s in range(SUBS):
        to_inner = pl.ds(pl.multiple_of(step * WIDE + s * LANES, LANES), LANES)
        inner[:, to_inner] = total_rows[pl.ds(s, length, stride=SUBS), :]


def final_kernel(length, modes, scale, inner, arrived, decay, residues, input_grad, resid_grad,
                 decay_grad):
    height = BACK * modes
    step = pl.program_id(0)
    remaining = (
        SUBS - lax.broadcasted_iota(jnp.int32, (SUBS, LANES), 0)
    ).astype(F32)
    tiles = decay.shape[1] // LANES
    for s in range(tiles):
        c = slice(s * LANES, (s + 1) * LANES)
        from_inner = pl.ds(pl.multiple_of((step * tiles + s) * LANES, LANES), LANES)
        at = (step * tiles + s) * height
        tail, chunk_factor = [], []
        for n in range(modes):
            rate = spread_cell(decay, n, c)
            carry = spread_row(arrived, at + n)
            tail.append(spread_cell(residues, n, c) * carry * jnp.exp(-rate * remaining))
            chunk_factor.append(jnp.exp(-rate * float(SUBS)))
        for low in range(length - 2 * SUBS, -1, -2 * SUBS):
            pair = []
            for begin in (low + SUBS, low):
                pair.append(inner[begin : begin + SUBS, from_inner] + pairwise(tail))
                tail = [f * z for f, z in zip(chunk_factor, tail)]
            input_grad[0, low : low + 2 * SUBS, c] = jnp.concatenate(pair[::-1], 0).astype(
                jnp.bfloat16
            )
        resid_grad[:, c] = arrived[rows(at + modes, modes), :] * scale
        decay_grad[:, c] = (
            -decay[:, c] * residues[:, c] * arrived[rows(at + 2 * modes, modes), :] * scale
        )


def on_device(values, gate_values, cotangent, residues, decay_rates):
    _, length, channels = values.shape
    modes = residues.shape[0]
    peers, rows_of = lax.axis_size("ctx"), lax.axis_size("dp")
    far = peers // NEAR
    wide = channels // WIDE
    assert modes == SUBS and wide == NEAR and far == SUBS and values.shape[0] == 1
    me = lax.axis_index("ctx")
    place = jnp.stack([me % NEAR, (me % NEAR) * SUBS + me // NEAR]).astype(jnp.int32)
    place, values = lax.optimization_barrier((place, values))
    near_groups = [[g * NEAR + k for k in range(NEAR)] for g in range(far)]
    far_groups = [[k * NEAR + g for k in range(far)] for g in range(NEAR)]
    shape = lambda *dims: jax.ShapeDtypeStruct(dims, F32)
    vmem = pl.BlockSpec(memory_space=pltpu.VMEM)
    smem = pl.BlockSpec(memory_space=pltpu.SMEM)
    on_chip = lambda x: pltpu.with_memory_space_constraint(x, pltpu.VMEM)
    held = lambda *dims: pltpu.VMEM(dims, F32)

    part = pl.BlockSpec((modes, channels // FINAL), lambda q: (0, q))
    small = pltpu.CompilerParams(vmem_limit_bytes=16 << 20)
    near_decay = on_chip(decay_rates)
    data = pl.BlockSpec((1, length, WIDE), lambda q: (0, 0, q))
    table = pl.BlockSpec((modes, WIDE), lambda q: (0, q))
    sent = pl.pallas_call(
        functools.partial(local_kernel, length, modes),
        grid=(wide,),
        in_specs=[data, data, data, table],
        out_specs=vmem,
        out_shape=held(wide * SUBS * SENT * modes, LANES),
        scratch_shapes=[pltpu.VMEM((SUBS * length, LANES), F32)] * 2,
        name="local",
    )(values, gate_values, cotangent, decay_rates)

    def exchange(x, axis, groups):
        return lax.all_to_all(x, axis, 0, 0, tiled=True, axis_index_groups=groups)

    near_data = exchange(sent.reshape(NEAR, SUBS * SENT * modes, LANES), "ctx", near_groups)
    inner = pl.pallas_call(
        functools.partial(inner_kernel, length, modes),
        grid=(wide,),
        in_specs=[data, data, table, table],
        out_specs=vmem,
        out_shape=held(length, channels),
        scratch_shapes=[pltpu.VMEM((length * SUBS, LANES), F32)] * 2
        + [pltpu.VMEM((modes * SUBS, LANES), F32)] * 2,
        cost_estimate=pl.CostEstimate(
            flops=4 * modes * length * channels,
            bytes_accessed=8 * length * channels,
            transcendentals=0,
        ),
        compiler_params=pltpu.CompilerParams(vmem_limit_bytes=60 << 20),
        name="inner",
    )(gate_values, cotangent, decay_rates, residues)
    totals, near_carries = pl.pallas_call(
        functools.partial(near_kernel, float(length), modes),
        in_specs=[smem, vmem, vmem],
        out_specs=[vmem, vmem],
        out_shape=[held(far, SENT * modes, LANES), held(NEAR, SUBS * modes, LANES)],
        name="near",
    )(place, near_decay, on_chip(near_data))

    far_data = exchange(totals, "ctx", far_groups)
    far_data, inner = lax.optimization_barrier((far_data, inner))
    far_carries, sums = pl.pallas_call(
        functools.partial(far_kernel, float(length * NEAR), modes),
        in_specs=[smem, vmem, vmem],
        out_specs=[vmem, vmem],
        out_shape=[held(far, modes, LANES), held(rows_of, 2 * modes, LANES)],
        name="far",
    )(place, near_decay, on_chip(far_data))

    all_sums = exchange(sums, "dp", None)
    far_out = pl.pallas_call(
        functools.partial(sum_kernel, modes),
        in_specs=[vmem, vmem],
        out_specs=vmem,
        out_shape=held(far, BACK * modes, LANES),
        name="sum",
    )(on_chip(far_carries), on_chip(all_sums))

    far_back = exchange(far_out, "ctx", far_groups)
    near_out = pl.pallas_call(
        functools.partial(spread_kernel, float(length), modes),
        in_specs=[smem, vmem, vmem, vmem],
        out_specs=vmem,
        out_shape=held(NEAR, SUBS * BACK * modes, LANES),
        name="spread",
    )(place, near_decay, on_chip(near_carries), on_chip(far_back))

    arrived = exchange(near_out, "ctx", near_groups)
    scale = 1.0 / math.sqrt(rows_of * length * peers)
    return pl.pallas_call(
        functools.partial(final_kernel, length, modes, scale),
        grid=(FINAL,),
        in_specs=[vmem, vmem, part, part],
        out_specs=[pl.BlockSpec((1, length, channels // FINAL), lambda q: (0, 0, q)), part, part],
        out_shape=[
            jax.ShapeDtypeStruct(values.shape, jnp.bfloat16),
            shape(modes, channels),
            shape(modes, channels),
        ],
        compiler_params=small,
        name="final",
    )(on_chip(inner), on_chip(arrived.reshape(-1, LANES)), decay_rates, residues)


def solution(mesh):
    return jax.shard_map(
        on_device,
        mesh=mesh,
        in_specs=(P("dp", "ctx", None), P("dp", "ctx", None), P("dp", "ctx", None), P(), P()),
        out_specs=(P("dp", "ctx", None), P(), P()),
        check_vma=False,
    )
```

```python
import functools
import math

import jax
import jax.numpy as jnp
from jax import lax
from jax.experimental import pallas as pl
from jax.experimental.pallas import tpu as pltpu
from jax.sharding import PartitionSpec as P

F32 = jnp.float32
LANES = 128
SUBS = 8
WIDE = LANES * SUBS
NEAR = 4
SENT = 6
BACK = 3
UNROLL = 8
FINAL = 2
TILES = 4


def rows(start, size):
    return pl.ds(pl.multiple_of(start, size), size)


def split_columns(read, scratch, length):
    for s in range(SUBS):
        scratch[pl.ds(s, length, stride=SUBS), :] = read(slice(s * LANES, (s + 1) * LANES))


def spread_row(ref, row):
    return ref[pl.ds(row, SUBS, stride=0), :]


def spread_cell(ref, row, columns):
    return jnp.broadcast_to(ref[row : row + 1, columns], (SUBS, LANES))


def local_kernel(length, modes, values, gate, cotangent, decay, sent, value_rows, grad_rows):
    height = SENT * modes
    step = pl.program_id(0)
    for s in range(SUBS):
        c, at = slice(s * LANES, (s + 1) * LANES), slice(s * length, (s + 1) * length)
        value_rows[at, :] = values[0, :, c].astype(F32)
        grad_rows[at, :] = cotangent[0, :, c].astype(F32) * gate[0, :, c].astype(F32)
    zero = jnp.zeros((modes, LANES), F32)
    for begin in range(0, SUBS, TILES):
        columns = [slice((begin + i) * LANES, (begin + i + 1) * LANES) for i in range(TILES)]
        factor = [jnp.exp(-decay[:, c]) for c in columns]

        def advance(chunk, carry):
            carry = [list(part) for part in carry]
            early = pl.multiple_of(chunk * SUBS, SUBS)
            late = pl.multiple_of(length - SUBS - chunk * SUBS, SUBS)
            for j in range(SUBS):
                for i in range(TILES):
                    first = (begin + i) * length
                    state, moment, back, ramp, sum0, sum1 = carry[i]
                    value_now = spread_row(value_rows, first + early + j)
                    grad_now = spread_row(grad_rows, first + early + j)
                    moment = factor[i] * (moment + state)
                    state = factor[i] * state + value_now
                    sum0 = sum0 + grad_now * state
                    sum1 = sum1 + grad_now * moment
                    ramp = factor[i] * (ramp + back)
                    back = factor[i] * back + spread_row(
                        grad_rows, first + late + SUBS - 1 - j
                    )
                    carry[i] = [state, moment, back, ramp, sum0, sum1]
            return carry

        carry = lax.fori_loop(0, length // SUBS, advance, [[zero] * SENT for _ in columns], unroll=4)
        for i, parts in enumerate(carry):
            for kind, part in enumerate(parts):
                at = (step * SUBS + begin + i) * height + kind * modes
                sent[rows(at, modes), :] = part


def joined(blocks, decay, span):
    factor = jnp.exp(-decay)
    fading = jnp.exp(-decay * span)
    zero = jnp.zeros_like(decay)
    carry, ramp, total0, total1 = zero, zero, zero, zero
    carries = []
    for state, moment, back, back_ramp, sum0, sum1 in reversed(blocks):
        carries.append(carry)
        near = factor * carry
        total0 = total0 + (sum0 + state * near)
        total1 = total1 + (sum1 + moment * near + state * (factor * ramp + near))
        ramp = fading * (ramp + span * carry) + back_ramp
        carry = fading * carry + back
    all_state, all_moment = zero, zero
    for state, moment, *_ in blocks:
        all_moment = fading * (all_moment + span * all_state) + moment
        all_state = fading * all_state + state
    return carries[::-1], (all_state, all_moment, carry, ramp, total0, total1)


def near_kernel(span, modes, place, decay, data, totals, carries):
    height = SENT * modes
    first = place[0] * WIDE
    for tile in range(SUBS):
        part = lambda b, k: data[b, tile * height + k * modes : tile * height + (k + 1) * modes, :]
        here = decay[:, pl.ds(pl.multiple_of(first + tile * LANES, LANES), LANES)]
        blocks = [[part(b, k) for k in range(SENT)] for b in range(data.shape[0])]
        before, total = joined(blocks, here, span)
        for b, carry in enumerate(before):
            carries[b, tile * modes : (tile + 1) * modes, :] = carry
        for k in range(SENT):
            totals[tile, k * modes : (k + 1) * modes, :] = total[k]


def far_kernel(span, modes, place, decay, data, carries, sums):
    here = decay[:, pl.ds(pl.multiple_of(place[1] * LANES, LANES), LANES)]
    blocks = [
        [data[b, k * modes : (k + 1) * modes, :] for k in range(SENT)] for b in range(data.shape[0])
    ]
    before, total = joined(blocks, here, span)
    for b, carry in enumerate(before):
        carries[b] = carry
    for d in range(sums.shape[0]):
        sums[d, :modes, :] = total[4]
        sums[d, modes:, :] = total[5]


def sum_kernel(modes, carries, sums, out):
    total = sums[0]
    for d in range(1, sums.shape[0]):
        total = total + sums[d]
    for b in range(out.shape[0]):
        out[b, :modes, :] = carries[b]
        out[b, modes:, :] = total


def spread_kernel(span, modes, place, decay, carries, far, out):
    height = BACK * modes
    first = place[0] * WIDE
    blocks = carries.shape[0]
    for tile in range(SUBS):
        here = decay[:, pl.ds(pl.multiple_of(first + tile * LANES, LANES), LANES)]
        fading = jnp.exp(-here * span)
        arriving = far[tile, :modes, :]
        for b in reversed(range(blocks)):
            start = tile * height
            out[b, start : start + modes, :] = (
                carries[b, tile * modes : (tile + 1) * modes, :] + arriving
            )
            out[b, start + modes : start + height, :] = far[tile, modes:, :]
            arriving = fading * arriving


def pairwise(terms):
    while len(terms) > 1:
        terms = [a + b for a, b in zip(terms[::2], terms[1::2])]
    return terms[0]


def inner_kernel(length, modes, gate, cotangent, decay, residues, inner, grad_rows, total_rows,
                 decay_rows, residue_rows):
    step = pl.program_id(0)
    split_columns(
        lambda c: cotangent[0, :, c].astype(F32) * gate[0, :, c].astype(F32), grad_rows, length
    )
    split_columns(lambda c: decay[:, c], decay_rows, modes)
    split_columns(lambda c: residues[:, c], residue_rows, modes)
    factor = [jnp.exp(-decay_rows[n * SUBS : (n + 1) * SUBS, :]) for n in range(modes)]
    weight = [residue_rows[n * SUBS : (n + 1) * SUBS, :] for n in range(modes)]

    def backward(k, back):
        at = rows((length - 1 - k) * SUBS, SUBS)
        grad_now = grad_rows[at, :]
        back = [factor[n] * back[n] + grad_now for n in range(modes)]
        total_rows[at, :] = pairwise([weight[n] * back[n] for n in range(modes)])
        return back

    lax.fori_loop(
        0, length, backward, [jnp.zeros((SUBS, LANES), F32)] * modes, unroll=UNROLL
    )
    for s in range(SUBS):
        to_inner = pl.ds(pl.multiple_of(step * WIDE + s * LANES, LANES), LANES)
        inner[:, to_inner] = total_rows[pl.ds(s, length, stride=SUBS), :]


def final_kernel(length, modes, scale, inner, arrived, decay, residues, input_grad, resid_grad,
                 decay_grad):
    height = BACK * modes
    step = pl.program_id(0)
    remaining = (
        SUBS - lax.broadcasted_iota(jnp.int32, (SUBS, LANES), 0)
    ).astype(F32)
    tiles = decay.shape[1] // LANES
    for s in range(tiles):
        c = slice(s * LANES, (s + 1) * LANES)
        from_inner = pl.ds(pl.multiple_of((step * tiles + s) * LANES, LANES), LANES)
        at = (step * tiles + s) * height
        tail, chunk_factor = [], []
        for n in range(modes):
            rate = spread_cell(decay, n, c)
            carry = spread_row(arrived, at + n)
            tail.append(spread_cell(residues, n, c) * carry * jnp.exp(-rate * remaining))
            chunk_factor.append(jnp.exp(-rate * float(SUBS)))
        for low in range(length - 2 * SUBS, -1, -2 * SUBS):
            pair = []
            for begin in (low + SUBS, low):
                pair.append(inner[begin : begin + SUBS, from_inner] + pairwise(tail))
                tail = [f * z for f, z in zip(chunk_factor, tail)]
            input_grad[0, low : low + 2 * SUBS, c] = jnp.concatenate(pair[::-1], 0).astype(
                jnp.bfloat16
            )
        resid_grad[:, c] = arrived[rows(at + modes, modes), :] * scale
        decay_grad[:, c] = (
            -decay[:, c] * residues[:, c] * arrived[rows(at + 2 * modes, modes), :] * scale
        )


def on_device(values, gate_values, cotangent, residues, decay_rates):
    _, length, channels = values.shape
    modes = residues.shape[0]
    peers, rows_of = lax.axis_size("ctx"), lax.axis_size("dp")
    far = peers // NEAR
    wide = channels // WIDE
    assert modes == SUBS and wide == NEAR and far == SUBS and values.shape[0] == 1
    me = lax.axis_index("ctx")
    place = jnp.stack([me % NEAR, (me % NEAR) * SUBS + me // NEAR]).astype(jnp.int32)
    place, values = lax.optimization_barrier((place, values))
    near_groups = [[g * NEAR + k for k in range(NEAR)] for g in range(far)]
    far_groups = [[k * NEAR + g for k in range(far)] for g in range(NEAR)]
    shape = lambda *dims: jax.ShapeDtypeStruct(dims, F32)
    vmem = pl.BlockSpec(memory_space=pltpu.VMEM)
    smem = pl.BlockSpec(memory_space=pltpu.SMEM)
    on_chip = lambda x: pltpu.with_memory_space_constraint(x, pltpu.VMEM)
    held = lambda *dims: pltpu.VMEM(dims, F32)

    part = pl.BlockSpec((modes, channels // FINAL), lambda q: (0, q))
    small = pltpu.CompilerParams(vmem_limit_bytes=16 << 20)
    near_decay = on_chip(decay_rates)
    data = pl.BlockSpec((1, length, WIDE), lambda q: (0, 0, q))
    table = pl.BlockSpec((modes, WIDE), lambda q: (0, q))
    sent = pl.pallas_call(
        functools.partial(local_kernel, length, modes),
        grid=(wide,),
        in_specs=[data, data, data, table],
        out_specs=vmem,
        out_shape=held(wide * SUBS * SENT * modes, LANES),
        scratch_shapes=[pltpu.VMEM((SUBS * length, LANES), F32)] * 2,
        name="local",
    )(values, gate_values, cotangent, decay_rates)

    def exchange(x, axis, groups):
        return lax.all_to_all(x, axis, 0, 0, tiled=True, axis_index_groups=groups)

    near_data = exchange(sent.reshape(NEAR, SUBS * SENT * modes, LANES), "ctx", near_groups)
    inner = pl.pallas_call(
        functools.partial(inner_kernel, length, modes),
        grid=(wide,),
        in_specs=[data, data, table, table],
        out_specs=vmem,
        out_shape=held(length, channels),
        scratch_shapes=[pltpu.VMEM((length * SUBS, LANES), F32)] * 2
        + [pltpu.VMEM((modes * SUBS, LANES), F32)] * 2,
        cost_estimate=pl.CostEstimate(
            flops=4 * modes * length * channels,
            bytes_accessed=8 * length * channels,
            transcendentals=0,
        ),
        compiler_params=pltpu.CompilerParams(vmem_limit_bytes=60 << 20),
        name="inner",
    )(gate_values, cotangent, decay_rates, residues)
    totals, near_carries = pl.pallas_call(
        functools.partial(near_kernel, float(length), modes),
        in_specs=[smem, vmem, vmem],
        out_specs=[vmem, vmem],
        out_shape=[held(far, SENT * modes, LANES), held(NEAR, SUBS * modes, LANES)],
        name="near",
    )(place, near_decay, on_chip(near_data))

    far_data = exchange(totals, "ctx", far_groups)
    far_carries, sums = pl.pallas_call(
        functools.partial(far_kernel, float(length * NEAR), modes),
        in_specs=[smem, vmem, vmem],
        out_specs=[vmem, vmem],
        out_shape=[held(far, modes, LANES), held(rows_of, 2 * modes, LANES)],
        name="far",
    )(place, near_decay, on_chip(far_data))

    all_sums = exchange(sums, "dp", None)
    far_out = pl.pallas_call(
        functools.partial(sum_kernel, modes),
        in_specs=[vmem, vmem],
        out_specs=vmem,
        out_shape=held(far, BACK * modes, LANES),
        name="sum",
    )(on_chip(far_carries), on_chip(all_sums))

    far_back = exchange(far_out, "ctx", far_groups)
    far_back, inner = lax.optimization_barrier((far_back, inner))
    near_out = pl.pallas_call(
        functools.partial(spread_kernel, float(length), modes),
        in_specs=[smem, vmem, vmem, vmem],
        out_specs=vmem,
        out_shape=held(NEAR, SUBS * BACK * modes, LANES),
        name="spread",
    )(place, near_decay, on_chip(near_carries), on_chip(far_back))

    arrived = exchange(near_out, "ctx", near_groups)
    scale = 1.0 / math.sqrt(rows_of * length * peers)
    return pl.pallas_call(
        functools.partial(final_kernel, length, modes, scale),
        grid=(FINAL,),
        in_specs=[vmem, vmem, part, part],
        out_specs=[pl.BlockSpec((1, length, channels // FINAL), lambda q: (0, 0, q)), part, part],
        out_shape=[
            jax.ShapeDtypeStruct(values.shape, jnp.bfloat16),
            shape(modes, channels),
            shape(modes, channels),
        ],
        compiler_params=small,
        name="final",
    )(on_chip(inner), on_chip(arrived.reshape(-1, LANES)), decay_rates, residues)


def solution(mesh):
    return jax.shard_map(
        on_device,
        mesh=mesh,
        in_specs=(P("dp", "ctx", None), P("dp", "ctx", None), P("dp", "ctx", None), P(), P()),
        out_specs=(P("dp", "ctx", None), P(), P()),
        check_vma=False,
    )
```

```python
import functools
import math

import jax
import jax.numpy as jnp
from jax import lax
from jax.experimental import pallas as pl
from jax.experimental.pallas import tpu as pltpu
from jax.sharding import PartitionSpec as P

F32 = jnp.float32
LANES = 128
SUBS = 8
WIDE = LANES * SUBS
NEAR = 4
SENT = 6
BACK = 3
UNROLL = 8
FINAL = 2
TILES = 4


def rows(start, size):
    return pl.ds(pl.multiple_of(start, size), size)


def split_columns(read, scratch, length):
    for s in range(SUBS):
        scratch[pl.ds(s, length, stride=SUBS), :] = read(slice(s * LANES, (s + 1) * LANES))


def spread_row(ref, row):
    return ref[pl.ds(row, SUBS, stride=0), :]


def spread_cell(ref, row, columns):
    return jnp.broadcast_to(ref[row : row + 1, columns], (SUBS, LANES))


def local_kernel(length, modes, values, gate, cotangent, decay, sent, value_rows, grad_rows):
    height = SENT * modes
    step = pl.program_id(0)
    for s in range(SUBS):
        c, at = slice(s * LANES, (s + 1) * LANES), slice(s * length, (s + 1) * length)
        value_rows[at, :] = values[0, :, c].astype(F32)
        grad_rows[at, :] = cotangent[0, :, c].astype(F32) * gate[0, :, c].astype(F32)
    zero = jnp.zeros((modes, LANES), F32)
    for begin in range(0, SUBS, TILES):
        columns = [slice((begin + i) * LANES, (begin + i + 1) * LANES) for i in range(TILES)]
        factor = [jnp.exp(-decay[:, c]) for c in columns]

        def advance(chunk, carry):
            carry = [list(part) for part in carry]
            early = pl.multiple_of(chunk * SUBS, SUBS)
            late = pl.multiple_of(length - SUBS - chunk * SUBS, SUBS)
            for j in range(SUBS):
                for i in range(TILES):
                    first = (begin + i) * length
                    state, moment, back, ramp, sum0, sum1 = carry[i]
                    value_now = spread_row(value_rows, first + early + j)
                    grad_now = spread_row(grad_rows, first + early + j)
                    moment = factor[i] * (moment + state)
                    state = factor[i] * state + value_now
                    sum0 = sum0 + grad_now * state
                    sum1 = sum1 + grad_now * moment
                    ramp = factor[i] * (ramp + back)
                    back = factor[i] * back + spread_row(
                        grad_rows, first + late + SUBS - 1 - j
                    )
                    carry[i] = [state, moment, back, ramp, sum0, sum1]
            return carry

        carry = lax.fori_loop(0, length // SUBS, advance, [[zero] * SENT for _ in columns], unroll=4)
        for i, parts in enumerate(carry):
            for kind, part in enumerate(parts):
                at = (step * SUBS + begin + i) * height + kind * modes
                sent[rows(at, modes), :] = part


def joined(blocks, decay, span):
    factor = jnp.exp(-decay)
    fading = jnp.exp(-decay * span)
    zero = jnp.zeros_like(decay)
    carry, ramp, total0, total1 = zero, zero, zero, zero
    carries = []
    for state, moment, back, back_ramp, sum0, sum1 in reversed(blocks):
        carries.append(carry)
        near = factor * carry
        total0 = total0 + (sum0 + state * near)
        total1 = total1 + (sum1 + moment * near + state * (factor * ramp + near))
        ramp = fading * (ramp + span * carry) + back_ramp
        carry = fading * carry + back
    all_state, all_moment = zero, zero
    for state, moment, *_ in blocks:
        all_moment = fading * (all_moment + span * all_state) + moment
        all_state = fading * all_state + state
    return carries[::-1], (all_state, all_moment, carry, ramp, total0, total1)


def near_kernel(span, modes, decay, data, totals, carries):
    height = SENT * modes
    first = lax.rem(lax.axis_index("ctx"), NEAR) * WIDE
    for tile in range(SUBS):
        part = lambda b, k: data[b, tile * height + k * modes : tile * height + (k + 1) * modes, :]
        here = decay[:, pl.ds(pl.multiple_of(first + tile * LANES, LANES), LANES)]
        blocks = [[part(b, k) for k in range(SENT)] for b in range(data.shape[0])]
        before, total = joined(blocks, here, span)
        for b, carry in enumerate(before):
            carries[b, tile * modes : (tile + 1) * modes, :] = carry
        for k in range(SENT):
            totals[tile, k * modes : (k + 1) * modes, :] = total[k]


def far_kernel(span, modes, decay, data, carries, sums):
    me = lax.axis_index("ctx")
    tile = lax.rem(me, NEAR) * SUBS + lax.div(me, NEAR)
    here = decay[:, pl.ds(pl.multiple_of(tile * LANES, LANES), LANES)]
    blocks = [
        [data[b, k * modes : (k + 1) * modes, :] for k in range(SENT)] for b in range(data.shape[0])
    ]
    before, total = joined(blocks, here, span)
    for b, carry in enumerate(before):
        carries[b] = carry
    for d in range(sums.shape[0]):
        sums[d, :modes, :] = total[4]
        sums[d, modes:, :] = total[5]


def sum_kernel(modes, carries, sums, out):
    total = sums[0]
    for d in range(1, sums.shape[0]):
        total = total + sums[d]
    for b in range(out.shape[0]):
        out[b, :modes, :] = carries[b]
        out[b, modes:, :] = total


def spread_kernel(span, modes, decay, carries, far, out):
    height = BACK * modes
    first = lax.rem(lax.axis_index("ctx"), NEAR) * WIDE
    blocks = carries.shape[0]
    for tile in range(SUBS):
        here = decay[:, pl.ds(pl.multiple_of(first + tile * LANES, LANES), LANES)]
        fading = jnp.exp(-here * span)
        arriving = far[tile, :modes, :]
        for b in reversed(range(blocks)):
            start = tile * height
            out[b, start : start + modes, :] = (
                carries[b, tile * modes : (tile + 1) * modes, :] + arriving
            )
            out[b, start + modes : start + height, :] = far[tile, modes:, :]
            arriving = fading * arriving


def pairwise(terms):
    while len(terms) > 1:
        terms = [a + b for a, b in zip(terms[::2], terms[1::2])]
    return terms[0]


def inner_kernel(length, modes, gate, cotangent, decay, residues, inner, grad_rows, total_rows,
                 decay_rows, residue_rows):
    step = pl.program_id(0)
    split_columns(
        lambda c: cotangent[0, :, c].astype(F32) * gate[0, :, c].astype(F32), grad_rows, length
    )
    split_columns(lambda c: decay[:, c], decay_rows, modes)
    split_columns(lambda c: residues[:, c], residue_rows, modes)
    factor = [jnp.exp(-decay_rows[n * SUBS : (n + 1) * SUBS, :]) for n in range(modes)]
    weight = [residue_rows[n * SUBS : (n + 1) * SUBS, :] for n in range(modes)]

    def backward(k, back):
        at = rows((length - 1 - k) * SUBS, SUBS)
        grad_now = grad_rows[at, :]
        back = [factor[n] * back[n] + grad_now for n in range(modes)]
        total_rows[at, :] = pairwise([weight[n] * back[n] for n in range(modes)])
        return back

    lax.fori_loop(
        0, length, backward, [jnp.zeros((SUBS, LANES), F32)] * modes, unroll=UNROLL
    )
    for s in range(SUBS):
        to_inner = pl.ds(pl.multiple_of(step * WIDE + s * LANES, LANES), LANES)
        inner[:, to_inner] = total_rows[pl.ds(s, length, stride=SUBS), :]


def final_kernel(length, modes, scale, inner, arrived, decay, residues, input_grad, resid_grad,
                 decay_grad):
    height = BACK * modes
    step = pl.program_id(0)
    remaining = (
        SUBS - lax.broadcasted_iota(jnp.int32, (SUBS, LANES), 0)
    ).astype(F32)
    tiles = decay.shape[1] // LANES
    for s in range(tiles):
        c = slice(s * LANES, (s + 1) * LANES)
        from_inner = pl.ds(pl.multiple_of((step * tiles + s) * LANES, LANES), LANES)
        at = (step * tiles + s) * height
        tail, chunk_factor = [], []
        for n in range(modes):
            rate = spread_cell(decay, n, c)
            carry = spread_row(arrived, at + n)
            tail.append(spread_cell(residues, n, c) * carry * jnp.exp(-rate * remaining))
            chunk_factor.append(jnp.exp(-rate * float(SUBS)))
        for low in range(length - 2 * SUBS, -1, -2 * SUBS):
            pair = []
            for begin in (low + SUBS, low):
                pair.append(inner[begin : begin + SUBS, from_inner] + pairwise(tail))
                tail = [f * z for f, z in zip(chunk_factor, tail)]
            input_grad[0, low : low + 2 * SUBS, c] = jnp.concatenate(pair[::-1], 0).astype(
                jnp.bfloat16
            )
        resid_grad[:, c] = arrived[rows(at + modes, modes), :] * scale
        decay_grad[:, c] = (
            -decay[:, c] * residues[:, c] * arrived[rows(at + 2 * modes, modes), :] * scale
        )


def on_device(values, gate_values, cotangent, residues, decay_rates):
    _, length, channels = values.shape
    modes = residues.shape[0]
    peers, rows_of = lax.axis_size("ctx"), lax.axis_size("dp")
    far = peers // NEAR
    wide = channels // WIDE
    assert modes == SUBS and wide == NEAR and far == SUBS and values.shape[0] == 1
    near_groups = [[g * NEAR + k for k in range(NEAR)] for g in range(far)]
    far_groups = [[k * NEAR + g for k in range(far)] for g in range(NEAR)]
    shape = lambda *dims: jax.ShapeDtypeStruct(dims, F32)
    vmem = pl.BlockSpec(memory_space=pltpu.VMEM)
    on_chip = lambda x: pltpu.with_memory_space_constraint(x, pltpu.VMEM)
    held = lambda *dims: pltpu.VMEM(dims, F32)

    part = pl.BlockSpec((modes, channels // FINAL), lambda q: (0, q))
    small = pltpu.CompilerParams(vmem_limit_bytes=16 << 20)
    near_decay = on_chip(decay_rates)
    data = pl.BlockSpec((1, length, WIDE), lambda q: (0, 0, q))
    table = pl.BlockSpec((modes, WIDE), lambda q: (0, q))
    sent = pl.pallas_call(
        functools.partial(local_kernel, length, modes),
        grid=(wide,),
        in_specs=[data, data, data, table],
        out_specs=vmem,
        out_shape=held(wide * SUBS * SENT * modes, LANES),
        scratch_shapes=[pltpu.VMEM((SUBS * length, LANES), F32)] * 2,
        name="local",
    )(values, gate_values, cotangent, decay_rates)

    def exchange(x, axis, groups):
        return lax.all_to_all(x, axis, 0, 0, tiled=True, axis_index_groups=groups)

    near_data = exchange(sent.reshape(NEAR, SUBS * SENT * modes, LANES), "ctx", near_groups)
    inner = pl.pallas_call(
        functools.partial(inner_kernel, length, modes),
        grid=(wide,),
        in_specs=[data, data, table, table],
        out_specs=vmem,
        out_shape=held(length, channels),
        scratch_shapes=[pltpu.VMEM((length * SUBS, LANES), F32)] * 2
        + [pltpu.VMEM((modes * SUBS, LANES), F32)] * 2,
        cost_estimate=pl.CostEstimate(
            flops=4 * modes * length * channels,
            bytes_accessed=8 * length * channels,
            transcendentals=0,
        ),
        compiler_params=pltpu.CompilerParams(vmem_limit_bytes=60 << 20),
        name="inner",
    )(gate_values, cotangent, decay_rates, residues)
    totals, near_carries = pl.pallas_call(
        functools.partial(near_kernel, float(length), modes),
        in_specs=[vmem, vmem],
        out_specs=[vmem, vmem],
        out_shape=[held(far, SENT * modes, LANES), held(NEAR, SUBS * modes, LANES)],
        name="near",
    )(near_decay, on_chip(near_data))

    far_data = exchange(totals, "ctx", far_groups)
    far_carries, sums = pl.pallas_call(
        functools.partial(far_kernel, float(length * NEAR), modes),
        in_specs=[vmem, vmem],
        out_specs=[vmem, vmem],
        out_shape=[held(far, modes, LANES), held(rows_of, 2 * modes, LANES)],
        name="far",
    )(near_decay, on_chip(far_data))

    all_sums = exchange(sums, "dp", None)
    far_out = pl.pallas_call(
        functools.partial(sum_kernel, modes),
        in_specs=[vmem, vmem],
        out_specs=vmem,
        out_shape=held(far, BACK * modes, LANES),
        name="sum",
    )(on_chip(far_carries), on_chip(all_sums))

    far_back = exchange(far_out, "ctx", far_groups)
    far_back, inner = lax.optimization_barrier((far_back, inner))
    near_out = pl.pallas_call(
        functools.partial(spread_kernel, float(length), modes),
        in_specs=[vmem, vmem, vmem],
        out_specs=vmem,
        out_shape=held(NEAR, SUBS * BACK * modes, LANES),
        name="spread",
    )(near_decay, on_chip(near_carries), on_chip(far_back))

    arrived = exchange(near_out, "ctx", near_groups)
    scale = 1.0 / math.sqrt(rows_of * length * peers)
    return pl.pallas_call(
        functools.partial(final_kernel, length, modes, scale),
        grid=(FINAL,),
        in_specs=[vmem, vmem, part, part],
        out_specs=[pl.BlockSpec((1, length, channels // FINAL), lambda q: (0, 0, q)), part, part],
        out_shape=[
            jax.ShapeDtypeStruct(values.shape, jnp.bfloat16),
            shape(modes, channels),
            shape(modes, channels),
        ],
        compiler_params=small,
        name="final",
    )(on_chip(inner), on_chip(arrived.reshape(-1, LANES)), decay_rates, residues)


def solution(mesh):
    return jax.shard_map(
        on_device,
        mesh=mesh,
        in_specs=(P("dp", "ctx", None), P("dp", "ctx", None), P("dp", "ctx", None), P(), P()),
        out_specs=(P("dp", "ctx", None), P(), P()),
        check_vma=False,
    )
```

```python
import functools
import math

import jax
import jax.numpy as jnp
from jax import lax
from jax.experimental import pallas as pl
from jax.experimental.pallas import tpu as pltpu
from jax.sharding import PartitionSpec as P

F32 = jnp.float32
LANES = 128
SUBS = 8
WIDE = LANES * SUBS
NEAR = 4
SENT = 6
BACK = 3
UNROLL = 8
FINAL = 2
TILES = 4


def rows(start, size):
    return pl.ds(pl.multiple_of(start, size), size)


def split_columns(read, scratch, length):
    for s in range(SUBS):
        scratch[pl.ds(s, length, stride=SUBS), :] = read(slice(s * LANES, (s + 1) * LANES))


def spread_row(ref, row):
    return ref[pl.ds(row, SUBS, stride=0), :]


def spread_cell(ref, row, columns):
    return jnp.broadcast_to(ref[row : row + 1, columns], (SUBS, LANES))


def local_kernel(length, modes, values, gate, cotangent, decay, sent, value_rows, grad_rows):
    height = SENT * modes
    step = pl.program_id(0)
    for s in range(SUBS):
        c, at = slice(s * LANES, (s + 1) * LANES), slice(s * length, (s + 1) * length)
        value_rows[at, :] = values[0, :, c].astype(F32)
        grad_rows[at, :] = cotangent[0, :, c].astype(F32) * gate[0, :, c].astype(F32)
    zero = jnp.zeros((modes, LANES), F32)
    for begin in range(0, SUBS, TILES):
        columns = [slice((begin + i) * LANES, (begin + i + 1) * LANES) for i in range(TILES)]
        factor = [jnp.exp(-decay[:, c]) for c in columns]

        def advance(chunk, carry):
            carry = [list(part) for part in carry]
            early = pl.multiple_of(chunk * SUBS, SUBS)
            late = pl.multiple_of(length - SUBS - chunk * SUBS, SUBS)
            for j in range(SUBS):
                for i in range(TILES):
                    first = (begin + i) * length
                    state, moment, back, ramp, sum0, sum1 = carry[i]
                    value_now = spread_row(value_rows, first + early + j)
                    grad_now = spread_row(grad_rows, first + early + j)
                    moment = factor[i] * (moment + state)
                    state = factor[i] * state + value_now
                    sum0 = sum0 + grad_now * state
                    sum1 = sum1 + grad_now * moment
                    ramp = factor[i] * (ramp + back)
                    back = factor[i] * back + spread_row(
                        grad_rows, first + late + SUBS - 1 - j
                    )
                    carry[i] = [state, moment, back, ramp, sum0, sum1]
            return carry

        carry = lax.fori_loop(0, length // SUBS, advance, [[zero] * SENT for _ in columns], unroll=4)
        for i, parts in enumerate(carry):
            for kind, part in enumerate(parts):
                at = (step * SUBS + begin + i) * height + kind * modes
                sent[rows(at, modes), :] = part


def joined(blocks, decay, span):
    factor = jnp.exp(-decay)
    fading = jnp.exp(-decay * span)
    zero = jnp.zeros_like(decay)
    carry, ramp, total0, total1 = zero, zero, zero, zero
    carries = []
    for state, moment, back, back_ramp, sum0, sum1 in reversed(blocks):
        carries.append(carry)
        near = factor * carry
        total0 = total0 + (sum0 + state * near)
        total1 = total1 + (sum1 + moment * near + state * (factor * ramp + near))
        ramp = fading * (ramp + span * carry) + back_ramp
        carry = fading * carry + back
    all_state, all_moment = zero, zero
    for state, moment, *_ in blocks:
        all_moment = fading * (all_moment + span * all_state) + moment
        all_state = fading * all_state + state
    return carries[::-1], (all_state, all_moment, carry, ramp, total0, total1)


def near_kernel(span, modes, decay, data, totals, carries):
    height = SENT * modes
    first = lax.rem(lax.axis_index("ctx"), NEAR) * WIDE
    for tile in range(SUBS):
        part = lambda b, k: data[b, tile * height + k * modes : tile * height + (k + 1) * modes, :]
        here = decay[:, pl.ds(pl.multiple_of(first + tile * LANES, LANES), LANES)]
        blocks = [[part(b, k) for k in range(SENT)] for b in range(data.shape[0])]
        before, total = joined(blocks, here, span)
        for b, carry in enumerate(before):
            carries[b, tile * modes : (tile + 1) * modes, :] = carry
        for k in range(SENT):
            totals[tile, k * modes : (k + 1) * modes, :] = total[k]


def far_kernel(span, modes, decay, data, carries, sums):
    me = lax.axis_index("ctx")
    tile = lax.rem(me, NEAR) * SUBS + lax.div(me, NEAR)
    here = decay[:, pl.ds(pl.multiple_of(tile * LANES, LANES), LANES)]
    blocks = [
        [data[b, k * modes : (k + 1) * modes, :] for k in range(SENT)] for b in range(data.shape[0])
    ]
    before, total = joined(blocks, here, span)
    for b, carry in enumerate(before):
        carries[b] = carry
    for d in range(sums.shape[0]):
        sums[d, :modes, :] = total[4]
        sums[d, modes:, :] = total[5]


def sum_kernel(modes, carries, sums, out):
    total = sums[0]
    for d in range(1, sums.shape[0]):
        total = total + sums[d]
    for b in range(out.shape[0]):
        out[b, :modes, :] = carries[b]
        out[b, modes:, :] = total


def spread_kernel(span, modes, decay, carries, far, out):
    height = BACK * modes
    first = lax.rem(lax.axis_index("ctx"), NEAR) * WIDE
    blocks = carries.shape[0]
    for tile in range(SUBS):
        here = decay[:, pl.ds(pl.multiple_of(first + tile * LANES, LANES), LANES)]
        fading = jnp.exp(-here * span)
        arriving = far[tile, :modes, :]
        for b in reversed(range(blocks)):
            start = tile * height
            out[b, start : start + modes, :] = (
                carries[b, tile * modes : (tile + 1) * modes, :] + arriving
            )
            out[b, start + modes : start + height, :] = far[tile, modes:, :]
            arriving = fading * arriving


def pairwise(terms):
    while len(terms) > 1:
        terms = [a + b for a, b in zip(terms[::2], terms[1::2])]
    return terms[0]


def inner_kernel(length, modes, gate, cotangent, decay, residues, inner, grad_rows, total_rows,
                 decay_rows, residue_rows):
    step = pl.program_id(0)
    split_columns(
        lambda c: cotangent[0, :, c].astype(F32) * gate[0, :, c].astype(F32), grad_rows, length
    )
    split_columns(lambda c: decay[:, c], decay_rows, modes)
    split_columns(lambda c: residues[:, c], residue_rows, modes)
    factor = [jnp.exp(-decay_rows[n * SUBS : (n + 1) * SUBS, :]) for n in range(modes)]
    weight = [residue_rows[n * SUBS : (n + 1) * SUBS, :] for n in range(modes)]

    def backward(k, back):
        at = rows((length - 1 - k) * SUBS, SUBS)
        grad_now = grad_rows[at, :]
        back = [factor[n] * back[n] + grad_now for n in range(modes)]
        total_rows[at, :] = pairwise([weight[n] * back[n] for n in range(modes)])
        return back

    lax.fori_loop(
        0, length, backward, [jnp.zeros((SUBS, LANES), F32)] * modes, unroll=UNROLL
    )
    for s in range(SUBS):
        to_inner = pl.ds(pl.multiple_of(step * WIDE + s * LANES, LANES), LANES)
        inner[:, to_inner] = total_rows[pl.ds(s, length, stride=SUBS), :]


def final_kernel(length, modes, scale, inner, arrived, decay, residues, input_grad, resid_grad,
                 decay_grad):
    height = BACK * modes
    step = pl.program_id(0)
    remaining = (
        SUBS - lax.broadcasted_iota(jnp.int32, (SUBS, LANES), 0)
    ).astype(F32)
    tiles = decay.shape[1] // LANES
    for s in range(tiles):
        c = slice(s * LANES, (s + 1) * LANES)
        from_inner = pl.ds(pl.multiple_of((step * tiles + s) * LANES, LANES), LANES)
        at = (step * tiles + s) * height
        tail, chunk_factor = [], []
        for n in range(modes):
            rate = spread_cell(decay, n, c)
            carry = spread_row(arrived, at + n)
            tail.append(spread_cell(residues, n, c) * carry * jnp.exp(-rate * remaining))
            chunk_factor.append(jnp.exp(-rate * float(SUBS)))
        for low in range(length - 2 * SUBS, -1, -2 * SUBS):
            pair = []
            for begin in (low + SUBS, low):
                pair.append(inner[begin : begin + SUBS, from_inner] + pairwise(tail))
                tail = [f * z for f, z in zip(chunk_factor, tail)]
            input_grad[0, low : low + 2 * SUBS, c] = jnp.concatenate(pair[::-1], 0).astype(
                jnp.bfloat16
            )
        resid_grad[:, c] = arrived[rows(at + modes, modes), :] * scale
        decay_grad[:, c] = (
            -decay[:, c] * residues[:, c] * arrived[rows(at + 2 * modes, modes), :] * scale
        )


def on_device(values, gate_values, cotangent, residues, decay_rates):
    _, length, channels = values.shape
    modes = residues.shape[0]
    peers, rows_of = lax.axis_size("ctx"), lax.axis_size("dp")
    far = peers // NEAR
    wide = channels // WIDE
    assert modes == SUBS and wide == NEAR and far == SUBS and values.shape[0] == 1
    near_groups = [[g * NEAR + k for k in range(NEAR)] for g in range(far)]
    far_groups = [[k * NEAR + g for k in range(far)] for g in range(NEAR)]
    shape = lambda *dims: jax.ShapeDtypeStruct(dims, F32)
    vmem = pl.BlockSpec(memory_space=pltpu.VMEM)
    on_chip = lambda x: pltpu.with_memory_space_constraint(x, pltpu.VMEM)
    held = lambda *dims: pltpu.VMEM(dims, F32)

    part = pl.BlockSpec((modes, channels // FINAL), lambda q: (0, q))
    small = pltpu.CompilerParams(vmem_limit_bytes=16 << 20)
    near_decay = on_chip(decay_rates)
    data = pl.BlockSpec((1, length, WIDE), lambda q: (0, 0, q))
    table = pl.BlockSpec((modes, WIDE), lambda q: (0, q))
    sent = pl.pallas_call(
        functools.partial(local_kernel, length, modes),
        grid=(wide,),
        in_specs=[data, data, data, table],
        out_specs=vmem,
        out_shape=held(wide * SUBS * SENT * modes, LANES),
        scratch_shapes=[pltpu.VMEM((SUBS * length, LANES), F32)] * 2,
        name="local",
    )(values, gate_values, cotangent, decay_rates)

    def exchange(x, axis, groups):
        return lax.all_to_all(x, axis, 0, 0, tiled=True, axis_index_groups=groups)

    near_data = exchange(sent.reshape(NEAR, SUBS * SENT * modes, LANES), "ctx", near_groups)
    inner = pl.pallas_call(
        functools.partial(inner_kernel, length, modes),
        grid=(wide,),
        in_specs=[data, data, table, table],
        out_specs=vmem,
        out_shape=held(length, channels),
        scratch_shapes=[pltpu.VMEM((length * SUBS, LANES), F32)] * 2
        + [pltpu.VMEM((modes * SUBS, LANES), F32)] * 2,
        cost_estimate=pl.CostEstimate(
            flops=4 * modes * length * channels,
            bytes_accessed=8 * length * channels,
            transcendentals=0,
        ),
        compiler_params=pltpu.CompilerParams(vmem_limit_bytes=60 << 20),
        name="inner",
    )(gate_values, cotangent, decay_rates, residues)
    totals, near_carries = pl.pallas_call(
        functools.partial(near_kernel, float(length), modes),
        in_specs=[vmem, vmem],
        out_specs=[vmem, vmem],
        out_shape=[held(far, SENT * modes, LANES), held(NEAR, SUBS * modes, LANES)],
        name="near",
    )(near_decay, on_chip(near_data))

    far_data = exchange(totals, "ctx", far_groups)
    far_carries, sums = pl.pallas_call(
        functools.partial(far_kernel, float(length * NEAR), modes),
        in_specs=[vmem, vmem],
        out_specs=[vmem, vmem],
        out_shape=[held(far, modes, LANES), held(rows_of, 2 * modes, LANES)],
        name="far",
    )(near_decay, on_chip(far_data))

    all_sums = exchange(sums, "dp", None)
    all_sums, inner = lax.optimization_barrier((all_sums, inner))
    far_out = pl.pallas_call(
        functools.partial(sum_kernel, modes),
        in_specs=[vmem, vmem],
        out_specs=vmem,
        out_shape=held(far, BACK * modes, LANES),
        name="sum",
    )(on_chip(far_carries), on_chip(all_sums))

    far_back = exchange(far_out, "ctx", far_groups)
    near_out = pl.pallas_call(
        functools.partial(spread_kernel, float(length), modes),
        in_specs=[vmem, vmem, vmem],
        out_specs=vmem,
        out_shape=held(NEAR, SUBS * BACK * modes, LANES),
        name="spread",
    )(near_decay, on_chip(near_carries), on_chip(far_back))

    arrived = exchange(near_out, "ctx", near_groups)
    scale = 1.0 / math.sqrt(rows_of * length * peers)
    return pl.pallas_call(
        functools.partial(final_kernel, length, modes, scale),
        grid=(FINAL,),
        in_specs=[vmem, vmem, part, part],
        out_specs=[pl.BlockSpec((1, length, channels // FINAL), lambda q: (0, 0, q)), part, part],
        out_shape=[
            jax.ShapeDtypeStruct(values.shape, jnp.bfloat16),
            shape(modes, channels),
            shape(modes, channels),
        ],
        compiler_params=small,
        name="final",
    )(on_chip(inner), on_chip(arrived.reshape(-1, LANES)), decay_rates, residues)


def solution(mesh):
    return jax.shard_map(
        on_device,
        mesh=mesh,
        in_specs=(P("dp", "ctx", None), P("dp", "ctx", None), P("dp", "ctx", None), P(), P()),
        out_specs=(P("dp", "ctx", None), P(), P()),
        check_vma=False,
    )
```

```python
import functools
import math

import jax
import jax.numpy as jnp
from jax import lax
from jax.experimental import pallas as pl
from jax.experimental.pallas import tpu as pltpu
from jax.sharding import PartitionSpec as P

F32 = jnp.float32
LANES = 128
SUBS = 8
WIDE = LANES * SUBS
NEAR = 4
SENT = 6
BACK = 3
UNROLL = 8
FINAL = 2
TILES = 4


def rows(start, size):
    return pl.ds(pl.multiple_of(start, size), size)


def split_columns(read, scratch, length):
    for s in range(SUBS):
        scratch[pl.ds(s, length, stride=SUBS), :] = read(slice(s * LANES, (s + 1) * LANES))


def spread_row(ref, row):
    return ref[pl.ds(row, SUBS, stride=0), :]


def spread_cell(ref, row, columns):
    return jnp.broadcast_to(ref[row : row + 1, columns], (SUBS, LANES))


def local_kernel(length, modes, values, gate, cotangent, decay, sent, value_rows, grad_rows):
    height = SENT * modes
    step = pl.program_id(0)
    for s in range(SUBS):
        c, at = slice(s * LANES, (s + 1) * LANES), slice(s * length, (s + 1) * length)
        value_rows[at, :] = values[0, :, c].astype(F32)
        grad_rows[at, :] = cotangent[0, :, c].astype(F32) * gate[0, :, c].astype(F32)
    zero = jnp.zeros((modes, LANES), F32)
    for begin in range(0, SUBS, TILES):
        columns = [slice((begin + i) * LANES, (begin + i + 1) * LANES) for i in range(TILES)]
        factor = [jnp.exp(-decay[:, c]) for c in columns]

        def advance(chunk, carry):
            carry = [list(part) for part in carry]
            early = pl.multiple_of(chunk * SUBS, SUBS)
            late = pl.multiple_of(length - SUBS - chunk * SUBS, SUBS)
            for j in range(SUBS):
                for i in range(TILES):
                    first = (begin + i) * length
                    state, moment, back, ramp, sum0, sum1 = carry[i]
                    value_now = spread_row(value_rows, first + early + j)
                    grad_now = spread_row(grad_rows, first + early + j)
                    moment = factor[i] * (moment + state)
                    state = factor[i] * state + value_now
                    sum0 = sum0 + grad_now * state
                    sum1 = sum1 + grad_now * moment
                    ramp = factor[i] * (ramp + back)
                    back = factor[i] * back + spread_row(
                        grad_rows, first + late + SUBS - 1 - j
                    )
                    carry[i] = [state, moment, back, ramp, sum0, sum1]
            return carry

        carry = lax.fori_loop(0, length // SUBS, advance, [[zero] * SENT for _ in columns], unroll=4)
        for i, parts in enumerate(carry):
            for kind, part in enumerate(parts):
                at = (step * SUBS + begin + i) * height + kind * modes
                sent[rows(at, modes), :] = part


def joined(blocks, decay, span):
    factor = jnp.exp(-decay)
    fading = jnp.exp(-decay * span)
    zero = jnp.zeros_like(decay)
    carry, ramp, total0, total1 = zero, zero, zero, zero
    carries = []
    for state, moment, back, back_ramp, sum0, sum1 in reversed(blocks):
        carries.append(carry)
        near = factor * carry
        total0 = total0 + (sum0 + state * near)
        total1 = total1 + (sum1 + moment * near + state * (factor * ramp + near))
        ramp = fading * (ramp + span * carry) + back_ramp
        carry = fading * carry + back
    all_state, all_moment = zero, zero
    for state, moment, *_ in blocks:
        all_moment = fading * (all_moment + span * all_state) + moment
        all_state = fading * all_state + state
    return carries[::-1], (all_state, all_moment, carry, ramp, total0, total1)


def near_kernel(span, modes, decay, data, totals, carries):
    height = SENT * modes
    first = lax.rem(lax.axis_index("ctx"), NEAR) * WIDE
    for tile in range(SUBS):
        part = lambda b, k: data[b, tile * height + k * modes : tile * height + (k + 1) * modes, :]
        here = decay[:, pl.ds(pl.multiple_of(first + tile * LANES, LANES), LANES)]
        blocks = [[part(b, k) for k in range(SENT)] for b in range(data.shape[0])]
        before, total = joined(blocks, here, span)
        for b, carry in enumerate(before):
            carries[b, tile * modes : (tile + 1) * modes, :] = carry
        for k in range(SENT):
            totals[tile, k * modes : (k + 1) * modes, :] = total[k]


def far_kernel(span, modes, decay, data, carries, sums):
    me = lax.axis_index("ctx")
    tile = lax.rem(me, NEAR) * SUBS + lax.div(me, NEAR)
    here = decay[:, pl.ds(pl.multiple_of(tile * LANES, LANES), LANES)]
    blocks = [
        [data[b, k * modes : (k + 1) * modes, :] for k in range(SENT)] for b in range(data.shape[0])
    ]
    before, total = joined(blocks, here, span)
    for b, carry in enumerate(before):
        carries[b] = carry
    for d in range(sums.shape[0]):
        sums[d, :modes, :] = total[4]
        sums[d, modes:, :] = total[5]


def sum_kernel(modes, carries, sums, out):
    total = sums[0]
    for d in range(1, sums.shape[0]):
        total = total + sums[d]
    for b in range(out.shape[0]):
        out[b, :modes, :] = carries[b]
        out[b, modes:, :] = total


def spread_kernel(span, modes, decay, carries, far, out):
    height = BACK * modes
    first = lax.rem(lax.axis_index("ctx"), NEAR) * WIDE
    blocks = carries.shape[0]
    for tile in range(SUBS):
        here = decay[:, pl.ds(pl.multiple_of(first + tile * LANES, LANES), LANES)]
        fading = jnp.exp(-here * span)
        arriving = far[tile, :modes, :]
        for b in reversed(range(blocks)):
            start = tile * height
            out[b, start : start + modes, :] = (
                carries[b, tile * modes : (tile + 1) * modes, :] + arriving
            )
            out[b, start + modes : start + height, :] = far[tile, modes:, :]
            arriving = fading * arriving


def pairwise(terms):
    while len(terms) > 1:
        terms = [a + b for a, b in zip(terms[::2], terms[1::2])]
    return terms[0]


def inner_kernel(length, modes, gate, cotangent, decay, residues, inner, grad_rows, total_rows,
                 decay_rows, residue_rows):
    step = pl.program_id(0)
    split_columns(
        lambda c: cotangent[0, :, c].astype(F32) * gate[0, :, c].astype(F32), grad_rows, length
    )
    split_columns(lambda c: decay[:, c], decay_rows, modes)
    split_columns(lambda c: residues[:, c], residue_rows, modes)
    factor = [jnp.exp(-decay_rows[n * SUBS : (n + 1) * SUBS, :]) for n in range(modes)]
    weight = [residue_rows[n * SUBS : (n + 1) * SUBS, :] for n in range(modes)]

    def backward(k, back):
        at = rows((length - 1 - k) * SUBS, SUBS)
        grad_now = grad_rows[at, :]
        back = [factor[n] * back[n] + grad_now for n in range(modes)]
        total_rows[at, :] = pairwise([weight[n] * back[n] for n in range(modes)])
        return back

    lax.fori_loop(
        0, length, backward, [jnp.zeros((SUBS, LANES), F32)] * modes, unroll=UNROLL
    )
    for s in range(SUBS):
        to_inner = pl.ds(pl.multiple_of(step * WIDE + s * LANES, LANES), LANES)
        inner[:, to_inner] = total_rows[pl.ds(s, length, stride=SUBS), :]


def final_kernel(length, modes, scale, inner, arrived, decay, residues, input_grad, resid_grad,
                 decay_grad):
    height = BACK * modes
    step = pl.program_id(0)
    remaining = (
        SUBS - lax.broadcasted_iota(jnp.int32, (SUBS, LANES), 0)
    ).astype(F32)
    tiles = decay.shape[1] // LANES
    for s in range(tiles):
        c = slice(s * LANES, (s + 1) * LANES)
        from_inner = pl.ds(pl.multiple_of((step * tiles + s) * LANES, LANES), LANES)
        at = (step * tiles + s) * height
        tail, chunk_factor = [], []
        for n in range(modes):
            rate = spread_cell(decay, n, c)
            carry = spread_row(arrived, at + n)
            tail.append(spread_cell(residues, n, c) * carry * jnp.exp(-rate * remaining))
            chunk_factor.append(jnp.exp(-rate * float(SUBS)))
        for low in range(length - 2 * SUBS, -1, -2 * SUBS):
            pair = []
            for begin in (low + SUBS, low):
                pair.append(inner[begin : begin + SUBS, from_inner] + pairwise(tail))
                tail = [f * z for f, z in zip(chunk_factor, tail)]
            input_grad[0, low : low + 2 * SUBS, c] = jnp.concatenate(pair[::-1], 0).astype(
                jnp.bfloat16
            )
        resid_grad[:, c] = arrived[rows(at + modes, modes), :] * scale
        decay_grad[:, c] = (
            -decay[:, c] * residues[:, c] * arrived[rows(at + 2 * modes, modes), :] * scale
        )


def on_device(values, gate_values, cotangent, residues, decay_rates):
    _, length, channels = values.shape
    modes = residues.shape[0]
    peers, rows_of = lax.axis_size("ctx"), lax.axis_size("dp")
    far = peers // NEAR
    wide = channels // WIDE
    assert modes == SUBS and wide == NEAR and far == SUBS and values.shape[0] == 1
    near_groups = [[g * NEAR + k for k in range(NEAR)] for g in range(far)]
    far_groups = [[k * NEAR + g for k in range(far)] for g in range(NEAR)]
    shape = lambda *dims: jax.ShapeDtypeStruct(dims, F32)
    vmem = pl.BlockSpec(memory_space=pltpu.VMEM)
    on_chip = lambda x: pltpu.with_memory_space_constraint(x, pltpu.VMEM)
    held = lambda *dims: pltpu.VMEM(dims, F32)

    part = pl.BlockSpec((modes, channels // FINAL), lambda q: (0, q))
    small = pltpu.CompilerParams(vmem_limit_bytes=16 << 20)
    near_decay = on_chip(decay_rates)
    data = pl.BlockSpec((1, length, WIDE), lambda q: (0, 0, q))
    table = pl.BlockSpec((modes, WIDE), lambda q: (0, q))
    sent = pl.pallas_call(
        functools.partial(local_kernel, length, modes),
        grid=(wide,),
        in_specs=[data, data, data, table],
        out_specs=vmem,
        out_shape=held(wide * SUBS * SENT * modes, LANES),
        scratch_shapes=[pltpu.VMEM((SUBS * length, LANES), F32)] * 2,
        name="local",
    )(values, gate_values, cotangent, decay_rates)

    def exchange(x, axis, groups):
        return lax.all_to_all(x, axis, 0, 0, tiled=True, axis_index_groups=groups)

    near_data = exchange(sent.reshape(NEAR, SUBS * SENT * modes, LANES), "ctx", near_groups)
    inner = pl.pallas_call(
        functools.partial(inner_kernel, length, modes),
        grid=(wide,),
        in_specs=[data, data, table, table],
        out_specs=vmem,
        out_shape=held(length, channels),
        scratch_shapes=[pltpu.VMEM((length * SUBS, LANES), F32)] * 2
        + [pltpu.VMEM((modes * SUBS, LANES), F32)] * 2,
        cost_estimate=pl.CostEstimate(
            flops=4 * modes * length * channels,
            bytes_accessed=8 * length * channels,
            transcendentals=0,
        ),
        compiler_params=pltpu.CompilerParams(vmem_limit_bytes=60 << 20),
        name="inner",
    )(gate_values, cotangent, decay_rates, residues)
    totals, near_carries = pl.pallas_call(
        functools.partial(near_kernel, float(length), modes),
        in_specs=[vmem, vmem],
        out_specs=[vmem, vmem],
        out_shape=[held(far, SENT * modes, LANES), held(NEAR, SUBS * modes, LANES)],
        name="near",
    )(near_decay, on_chip(near_data))

    far_data = exchange(totals, "ctx", far_groups)
    far_data, inner = lax.optimization_barrier((far_data, inner))
    far_carries, sums = pl.pallas_call(
        functools.partial(far_kernel, float(length * NEAR), modes),
        in_specs=[vmem, vmem],
        out_specs=[vmem, vmem],
        out_shape=[held(far, modes, LANES), held(rows_of, 2 * modes, LANES)],
        name="far",
    )(near_decay, on_chip(far_data))

    all_sums = exchange(sums, "dp", None)
    far_out = pl.pallas_call(
        functools.partial(sum_kernel, modes),
        in_specs=[vmem, vmem],
        out_specs=vmem,
        out_shape=held(far, BACK * modes, LANES),
        name="sum",
    )(on_chip(far_carries), on_chip(all_sums))

    far_back = exchange(far_out, "ctx", far_groups)
    near_out = pl.pallas_call(
        functools.partial(spread_kernel, float(length), modes),
        in_specs=[vmem, vmem, vmem],
        out_specs=vmem,
        out_shape=held(NEAR, SUBS * BACK * modes, LANES),
        name="spread",
    )(near_decay, on_chip(near_carries), on_chip(far_back))

    arrived = exchange(near_out, "ctx", near_groups)
    scale = 1.0 / math.sqrt(rows_of * length * peers)
    return pl.pallas_call(
        functools.partial(final_kernel, length, modes, scale),
        grid=(FINAL,),
        in_specs=[vmem, vmem, part, part],
        out_specs=[pl.BlockSpec((1, length, channels // FINAL), lambda q: (0, 0, q)), part, part],
        out_shape=[
            jax.ShapeDtypeStruct(values.shape, jnp.bfloat16),
            shape(modes, channels),
            shape(modes, channels),
        ],
        compiler_params=small,
        name="final",
    )(on_chip(inner), on_chip(arrived.reshape(-1, LANES)), decay_rates, residues)


def solution(mesh):
    return jax.shard_map(
        on_device,
        mesh=mesh,
        in_specs=(P("dp", "ctx", None), P("dp", "ctx", None), P("dp", "ctx", None), P(), P()),
        out_specs=(P("dp", "ctx", None), P(), P()),
        check_vma=False,
    )
```
